128 devices in a mesh: dp: 8 (over z, y_lo), space: 16 (over x, y_hi, core).
Axes of the slice: x: 4, y: 4 (y_hi: 2, y_lo: 2; y = y_hi * 2 + y_lo), z: 4, core: 2. Of those that a mesh axis runs over, the one named last changes fastest.
Arguments:
- inputs: bfloat16 [112, 32, 32, 640], P('dp', 'space'), may hold values from -27 to 27
- norm_gain: float32 [640], replicated, may hold values from 0.1 to 1.9
- norm_bias: float32 [640], replicated, may hold values from -3 to 3
- conv_weight: bfloat16 [9, 640, 640], P(None, 'dp'), may hold values from -0.078125 to 0.078125
- upstream: bfloat16 [112, 32, 32, 640], P('dp', 'space'), may hold values from -6 to 6
Outputs:
- mixed: bfloat16 [112, 32, 32, 640], P('dp', 'space')
- input_grad: bfloat16 [112, 32, 32, 640], P('dp', 'space')
- weight_grad: float32 [9, 640, 640], P(None, 'dp', 'space')
- gain_grad: float32 [640], replicated
- bias_grad: float32 [640], replicated
The draws below stay inside these ranges and needn't reach their ends.
All inputs are finite; a program needn't handle non-finite values.
Results may differ from the reference program's by a relative error of at most 0.0031.
Values may be sent and summed in bfloat16 or wider, within the bound.
A program may use at most 128 MiB of HBM per device.

```python
import jax
import jax.numpy as jnp
from jax import lax

C = 640
GSIZE = 40
WIDTH = 32
HEIGHT = 32
IMAGES = 112


def draw_inputs(key, part):
    noise_key, scale_key = jax.random.split(key, 2)
    heights = jnp.arange(HEIGHT, dtype=jnp.float32) / max(HEIGHT - 1, 1)
    rising = 0.5 * jnp.exp(heights * jnp.log(3.0))
    channel_scale = jnp.exp(jax.random.uniform(scale_key, (IMAGES, 1, 1, C), jnp.float32, jnp.log(0.3), jnp.log(3.0)))
    values = jnp.clip(jax.random.normal(noise_key, (IMAGES, HEIGHT, WIDTH, C), jnp.float32), -6.0, 6.0)
    return (values * rising[None, :, None, None] * channel_scale).astype(jnp.bfloat16)


def with_spikes(entries, key, source, target, shards_of, factor):
    def block_of(axis_at):
        return (jnp.arange(entries.shape[axis_at]) // (entries.shape[axis_at] // shards_of)).reshape((-1,) + (1,) * (entries.ndim - 1 - axis_at))

    first = jax.random.permutation(key, shards_of)[block_of(target)]
    second = (block_of(target) + shards_of // 2) % shards_of
    return jnp.where((block_of(source) == first) | (block_of(source) == second), factor * entries, entries)


def level_of(own_key, dims, cuts, least, largest):
    factor_of, own = 1.0, jax.random.fold_in(own_key, 6)
    for position, shards_of in cuts:
        steps = jnp.exp(jax.random.uniform(jax.random.fold_in(own, position), (shards_of,), jnp.float32, least / len(cuts), largest / len(cuts)))
        factor_of = factor_of * jnp.repeat(steps, dims[position] // shards_of).reshape([-1 if axis == position else 1 for axis in range(len(dims))])
    return factor_of


def noise(stream_key, dims, deviation, most, shards=(), held_as=jnp.bfloat16):
    values = deviation * jax.random.normal(stream_key, dims, jnp.float32)
    if shards:
        values = values * level_of(stream_key, dims, shards, -0.22, 0.18)
    return jnp.clip(values, -most, most).astype(held_as)


def noise_with(stream_key, dims, width, bound, cuts, heavy, held_as=jnp.bfloat16):
    result = width * jax.random.normal(stream_key, dims, jnp.float32)
    if cuts:
        result = result * level_of(stream_key, dims, cuts, -0.22, 0.18)
    return jnp.clip(with_spikes(result, jax.random.fold_in(stream_key, 3), *heavy), -bound, bound).astype(held_as)


def setup_inputs(seed: int = 0) -> dict:
    key_of = jax.random.split(jax.random.key(seed), 6)
    return {
        "inputs": draw_inputs(jax.random.fold_in(key_of[5], 71), 0),
        "norm_gain": jnp.clip(1.0 + 0.18 * jax.random.normal(key_of[1], (C,), jnp.float32), 0.1, 1.9),
        "norm_bias": noise(key_of[2], (C,), 0.5, 3.0, (), jnp.float32),
        "conv_weight": noise(key_of[3], (9, C, C), (9 * C) ** -0.5, 0.078125, ((1, 8),)),
        "upstream": noise_with(key_of[4], (IMAGES, HEIGHT, WIDTH, C), 1.0, 6.0, ((0, 8), (1, 16)), (1, 3, 16, 2.0)),
    }


EPS = 1e-05

def group_means(values, count):
    image_count, height_all, width_all, channels = values.shape
    grouped = values.reshape(image_count, height_all, width_all, channels // GSIZE, GSIZE)
    return lax.optimization_barrier(jnp.sum(grouped, axis=(1, 2, 4))) / count

def spread_groups(group_vals):
    return jnp.repeat(group_vals, GSIZE, axis=1)[:, None, None, :]

def reference(inputs, norm_gain, norm_bias, conv_weight, upstream):
    x_float = inputs.astype(jnp.float32)
    image_count, height_all, width_all, channels = x_float.shape
    count = float(height_all * width_all * GSIZE)
    group_mean = group_means(x_float, count)
    group_square = group_means(x_float * x_float, count)
    group_rstd = lax.rsqrt(group_square - group_mean * group_mean + EPS)
    mean_chan = spread_groups(group_mean)
    rstd_chan = spread_groups(group_rstd)
    centred = (x_float - mean_chan) * rstd_chan
    normed = centred * norm_gain + norm_bias
    activated = jax.nn.silu(normed).astype(jnp.bfloat16)
    act_pad = jnp.pad(activated, ((0, 0), (1, 1), (1, 1), (0, 0)))
    grad_pad = jnp.pad(upstream, ((0, 0), (1, 1), (1, 1), (0, 0)))
    upstream_flat = upstream.reshape(-1, channels)
    conv_out = jnp.zeros((upstream_flat.shape[0], channels), jnp.float32)
    act_grad = jnp.zeros((upstream_flat.shape[0], channels), jnp.float32)
    grad_list = []
    for tap_row in range(3):
        for tap_col in range(3):
            tap_index = 3 * tap_row + tap_col
            act_window = act_pad[:, tap_row:tap_row + height_all, tap_col:tap_col + width_all, :].reshape(-1, channels)
            grad_window = grad_pad[:, 2 - tap_row:2 - tap_row + height_all, 2 - tap_col:2 - tap_col + width_all, :].reshape(-1, channels)
            conv_out = conv_out + jnp.dot(act_window, conv_weight[tap_index], preferred_element_type=jnp.float32)
            act_grad = act_grad + jnp.dot(grad_window, conv_weight[tap_index].T, preferred_element_type=jnp.float32)
            grad_list.append(jnp.dot(act_window.T, upstream_flat, preferred_element_type=jnp.float32))
    mixed = (x_float + conv_out.reshape(x_float.shape)).astype(jnp.bfloat16)
    weight_grad = jnp.stack(grad_list)
    sigmoid_n = jax.nn.sigmoid(normed)
    normed_grad = act_grad.reshape(x_float.shape) * sigmoid_n * (1.0 + normed * (1.0 - sigmoid_n))
    gain_grad = lax.optimization_barrier(jnp.sum(normed_grad * centred, axis=(0, 1, 2)))
    bias_grad = lax.optimization_barrier(jnp.sum(normed_grad, axis=(0, 1, 2)))
    centred_grad = normed_grad * norm_gain
    first_mean = spread_groups(group_means(centred_grad, count))
    second_mean = spread_groups(group_means(centred_grad * centred, count))
    input_grad = (upstream.astype(jnp.float32) + rstd_chan * (centred_grad - first_mean - centred * second_mean)).astype(jnp.bfloat16)
    return (mixed, input_grad, weight_grad, gain_grad, bias_grad)
```

```python
import functools

import jax
import jax.numpy as jnp
from jax import lax
from jax.experimental import pallas as pl
from jax.experimental.pallas import tpu as pltpu
from jax.sharding import PartitionSpec as P

GSIZE = 40
EPS = 1e-05
MESH = pl.DeviceIdType.MESH
NIMG = 14
COLS = 32
CH = 640
PIX = NIMG * COLS
OWN = 2 * PIX
COUNT = float(32 * 32 * GSIZE)
F32 = jnp.float32
BF16 = jnp.bfloat16
HIGH = lax.Precision.HIGHEST


def rcopy(src, dst, ssem, rsem, dev):
    return pltpu.make_async_remote_copy(
        src_ref=src, dst_ref=dst, send_sem=ssem, recv_sem=rsem, device_id=dev, device_id_type=MESH
    )


def al(value, unit):
    return pl.multiple_of(value, unit)


def sigmoid(v):
    return 1.0 / (1.0 + jnp.exp(-v))


def kernel(
    x_ref, gain_ref, bias_ref, w_ref, up_ref,
    mixed_ref, ig_ref, wg_ref, gb_ref,
    xh, uh, A3, U3, aT, W, sib_s, sib_r, s1, r1, x2s, x2r, y2s, y2r, ng,
    chs, mcs, st_s, st_r, bst_s, bst_r, gb_s, gb_r, gb2_r,
    st_ss, st_rs, bst_ss, bst_rs, gb_ss, gb_rs, gb2_ss, gb2_rs,
    h_ss, h_rs, ag_ss, ag_rs, ax_ss, ax_rs, fw_ss, fw_rs,
    sib_ss, sib_rs, z_ss, z_rs, x2_ss, x2_rs, y2_ss, y2_rs,
):
    dp = lax.axis_index("dp")
    s = lax.axis_index("space")
    x = lax.div(s, 4)
    yhi = lax.rem(lax.div(s, 2), 2)
    c = lax.rem(s, 2)
    z = lax.div(dp, 2)
    ylo = lax.rem(dp, 2)
    y = yhi * 2 + ylo
    sib = (dp, s + 1 - 2 * c)

    def zdev(k):
        return (lax.rem(z + k, 4) * 2 + ylo, s)

    def xdev(k):
        return (dp, lax.rem(s + 4 * k, 16))

    bar = pltpu.get_barrier_semaphore()

    def greet_space(k, _):
        pl.semaphore_signal(bar, inc=1, device_id=(dp, lax.rem(s + k, 16)), device_id_type=MESH)
        return 0

    def greet_dp(k, _):
        pl.semaphore_signal(bar, inc=1, device_id=(lax.rem(dp + k, 8), s), device_id_type=MESH)
        return 0

    lax.fori_loop(1, 16, greet_space, 0)
    lax.fori_loop(1, 8, greet_dp, 0)
    for a, b in ((0, 1), (1, 0), (1, 1)):
        other = (x * 2 + lax.rem(yhi + a, 2)) * 2 + lax.rem(c + b, 2)
        pl.semaphore_signal(bar, inc=1, device_id=(z * 2 + 1 - ylo, other), device_id_type=MESH)

    def table(shape, chan_dim, shift):
        chan = lax.broadcasted_iota(jnp.int32, shape, chan_dim)
        lane = lax.broadcasted_iota(jnp.int32, shape, 1 - chan_dim) - shift
        return jnp.where((chan >= lane * GSIZE) & (chan < (lane + 1) * GSIZE), 1.0, 0.0).astype(F32)

    def to_groups(first, second):
        return jnp.dot(first, table((CH, 128), 0, 0), precision=HIGH, preferred_element_type=F32) + jnp.dot(
            second, table((CH, 128), 0, 16), precision=HIGH, preferred_element_type=F32
        )

    def to_chans(vals, shift):
        return jnp.dot(vals, table((128, CH), 1, shift), precision=HIGH, preferred_element_type=F32) / COUNT

    chs[...] = jnp.zeros_like(chs)

    def stat_step(n, _):
        v = x_ref[n].astype(F32).reshape(2 * COLS, CH)
        chs[0, pl.ds(n, 1), :] = jnp.sum(v, axis=0, keepdims=True)
        chs[1, pl.ds(n, 1), :] = jnp.sum(v * v, axis=0, keepdims=True)
        return 0

    lax.fori_loop(0, NIMG, stat_step, 0)
    stats = to_groups(chs[0], chs[1])
    st_s[...] = stats
    tb = 2 * x + c
    W[pl.ds(al(tb * CH + dp * 80, 16), 80), :] = w_ref[tb]
    W[pl.ds(al(8 * CH + dp * 80, 16), 80), :] = w_ref[8]
    pl.semaphore_wait(bar, 25)

    def sp_copy(src, dst, ssem, rsem, k):
        return rcopy(src, dst.at[s], ssem.at[k], rsem.at[s], (dp, lax.rem(s + k, 16)))

    def sp_start(src, dst, ssem, rsem):
        def step(k, _):
            sp_copy(src, dst, ssem, rsem, k).start()
            return 0

        lax.fori_loop(1, 16, step, 0)
        dst[s] = src[...]

    def sp_wait(src, dst, ssem, rsem):
        def step(k, _):
            slot = lax.rem(s + k, 16)
            rcopy(src, dst.at[slot], ssem.at[k], rsem.at[slot], (dp, slot)).wait_recv()
            return 0

        lax.fori_loop(1, 16, step, 0)

    def sp_drain(src, dst, ssem, rsem):
        def step(k, _):
            sp_copy(src, dst, ssem, rsem, k).wait_send()
            return 0

        lax.fori_loop(1, 16, step, 0)

    st = (st_s, st_r, st_ss, st_rs)
    sp_start(*st)

    def wrows(tap, block):
        return W.at[pl.ds(al(tap * CH + block * 80, 16), 80), :]

    dy = 1 - 2 * c
    yto = lax.rem(y + dy + 4, 4)
    ydev = (z * 2 + lax.rem(yto, 2), (x * 2 + lax.div(yto, 2)) * 2 + c)
    dpo = z * 2 + 1 - ylo

    def ag_y(j):
        tap = tb if j == 0 else 8
        return rcopy(w_ref.at[tap], wrows(tap, dp), ag_ss.at[j], ag_rs.at[j], ydev)

    def ag_z(k, j, relay):
        tap = tb if j == 0 else 8
        idx = 2 + 2 * (k - 1) + j + (6 if relay else 0)
        src = wrows(tap, dpo) if relay else w_ref.at[tap]
        return rcopy(src, wrows(tap, dpo if relay else dp), ag_ss.at[idx], ag_rs.at[idx], zdev(k))

    def ag_y_recv(j):
        tap = tb if j == 0 else 8
        return rcopy(w_ref.at[tap], wrows(tap, dpo), ag_ss.at[j], ag_rs.at[j], ydev)

    def ag_z_recv(k, j, relay):
        tap = tb if j == 0 else 8
        idx = 2 + 2 * (k - 1) + j + (6 if relay else 0)
        zs = lax.rem(z + 4 - k, 4)
        block = zs * 2 + (1 - ylo if relay else ylo)
        return rcopy(w_ref.at[tap], wrows(tap, block), ag_ss.at[idx], ag_rs.at[idx], zdev(k))

    for j in range(2):
        ag_y(j).start()
        for k in (1, 3, 2):
            ag_z(k, j, False).start()

    above = (dp, lax.rem(s + 15, 16))
    below = (dp, lax.rem(s + 1, 16))

    def halo(i):
        ref, dst = (up_ref, uh) if i < 2 else (x_ref, xh)
        if i % 2 == 0:
            return rcopy(ref.at[:, 0], dst.at[1], h_ss.at[i], h_rs.at[i], above)
        return rcopy(ref.at[:, 1], dst.at[0], h_ss.at[i], h_rs.at[i], below)

    for i in range(4):
        halo(i).start()

    def put3(dst, row, n, v, flip):
        at = pl.ds(al(row * PIX + n * COLS, 32), COLS)
        col = lax.broadcasted_iota(jnp.int32, (COLS, CH), 0)
        prev = jnp.where(col == 0, 0.0, pltpu.roll(v, 1, 0))
        after = jnp.where(col == COLS - 1, 0.0, pltpu.roll(v, COLS - 1, 0))
        first, last = (after, prev) if flip else (prev, after)
        dst[at, 0:CH] = first.astype(BF16)
        dst[at, CH : 2 * CH] = v.astype(BF16)
        dst[at, 2 * CH : 3 * CH] = last.astype(BF16)

    def up_own(n, _):
        for r in range(2):
            put3(U3, r + 1, n, up_ref[n, r].astype(F32), True)
        return 0

    lax.fori_loop(0, NIMG, up_own, 0)

    for j in range(2):
        ag_y_recv(j).wait_recv()
        for k in (1, 3, 2):
            ag_z(k, j, True).start()

    sp_wait(*st)

    def slot_sum(ref):
        total = ref[0]
        for i in range(1, ref.shape[0]):
            total = total + ref[i]
        return total

    tot = slot_sum(st_r)
    mean = to_chans(tot, 0)
    mcs[0] = mean
    mcs[1] = lax.rsqrt(to_chans(tot, 16) - mean * mean + EPS)
    gain = gain_ref[...]
    bias = bias_ref[...]

    def centred_of(v, n):
        return (v - mcs[0, pl.ds(n, 1), :]) * mcs[1, pl.ds(n, 1), :]

    def act_of(v, n):
        normed = centred_of(v, n) * gain + bias
        return normed * sigmoid(normed)

    def act_own(n, _):
        for r in range(2):
            put3(A3, r + 1, n, act_of(x_ref[n, r].astype(F32), n), False)
        return 0

    lax.fori_loop(0, NIMG, act_own, 0)

    def turn(m, _):
        block = A3[pl.ds(al(PIX + m * 128, 16), 128), CH : 2 * CH].astype(F32).T.astype(BF16)
        for q in range(4):
            for p in range(2):
                d = 2 * q + p
                aT[p, q * 80 : (q + 1) * 80, pl.ds(al(m * 128, 128), 128)] = block[d * 80 : (d + 1) * 80]
        return 0

    lax.fori_loop(0, OWN // 128, turn, 0)

    for k in (1, 3, 2):
        ag_z_recv(k, 0, False).wait_recv()
        ag_z_recv(k, 0, True).wait_recv()

    def tap_rows(tap):
        return W.at[pl.ds(al(tap * CH, 16), CH), :]

    def ax(k):
        return rcopy(tap_rows(tb), tap_rows(tb), ax_ss.at[k - 1], ax_rs.at[k - 1], xdev(k))

    def ax_recv(k):
        tap = 2 * lax.rem(x + 4 - k, 4) + c
        return rcopy(tap_rows(tap), tap_rows(tap), ax_ss.at[k - 1], ax_rs.at[k - 1], xdev(k))

    def fw(k):
        tap = 2 * lax.rem(x + 4 - k, 4) + c
        return rcopy(tap_rows(tap), tap_rows(tap), fw_ss.at[k], fw_rs.at[k], sib)

    def fw_recv(k):
        tap = 2 * lax.rem(x + 4 - k, 4) + 1 - c
        return rcopy(tap_rows(tap), tap_rows(tap), fw_ss.at[k], fw_rs.at[k], sib)

    for k in (1, 3, 2):
        ax(k).start()
    fw(0).start()

    for i in range(2):
        halo(i).wait_recv()

    def masked(v, edge):
        return jnp.where(s == (0 if edge == 0 else 15), jnp.zeros_like(v), v)

    def up_halo(n, _):
        for e in range(2):
            put3(U3, 3 * e, n, masked(uh[e, n].astype(F32), e), True)
        return 0

    lax.fori_loop(0, NIMG, up_halo, 0)

    def terms(p, dr, dc):
        rhs = U3[pl.ds(al((2 - dr) * PIX, 16), OWN), dc * CH : (dc + 1) * CH]
        return jnp.dot(aT[p], rhs, preferred_element_type=F32)

    def sib_copy(t):
        return rcopy(sib_s.at[t], sib_r.at[t], sib_ss.at[t], sib_rs.at[t], sib)

    def far_step(dr, _):
        for dc in range(3):
            t = 3 * dr + dc
            sib_s[t] = terms(1 - c, dr, dc).astype(BF16)
            sib_copy(t).start()
        return 0

    lax.fori_loop(0, 3, far_step, 0)

    def zsum(g, k):
        to = lax.rem(z + k, 4)
        return rcopy(
            s1.at[pl.ds(3 * g, 3), to], r1.at[g, k - 1], z_ss.at[3 * g + k - 1], z_rs.at[3 * g + k - 1], zdev(k)
        )

    def near_step(dr, _):
        for dc in range(3):
            t = 3 * dr + dc
            own = terms(c, dr, dc)
            sib_copy(t).wait_recv()
            s1[t] = (own + sib_r[t].astype(F32)).astype(BF16).reshape(4, 80, CH)
        for k in (1, 3, 2):
            zsum(dr, k).start()
        return 0

    lax.fori_loop(0, 3, near_step, 0)

    for i in range(2, 4):
        halo(i).wait_recv()

    def act_halo(n, _):
        for e in range(2):
            put3(A3, 3 * e, n, masked(act_of(xh[e, n].astype(F32), n), e), False)
        return 0

    lax.fori_loop(0, NIMG, act_halo, 0)

    for k in (1, 3, 2):
        ax_recv(k).wait_recv()
        fw(k).start()
    for k in (1, 3, 2):
        ag_z_recv(k, 1, False).wait_recv()
        ag_z_recv(k, 1, True).wait_recv()
    for k in (0, 1, 3, 2):
        fw_recv(k).wait_recv()

    def conv_step(r, _):
        total = None
        for dr in range(3):
            part = jnp.dot(
                A3[pl.ds(al((r + dr) * PIX, 16), PIX), :],
                W[dr * 3 * CH : (dr + 1) * 3 * CH, :],
                preferred_element_type=F32,
            )
            total = part if total is None else total + part
        ng[pl.ds(al(r * PIX, 16), PIX), :] = total
        return 0

    lax.fori_loop(0, 2, conv_step, 0)

    def mix_step(n, _):
        for r in range(2):
            at = pl.ds(al(r * PIX + n * COLS, 32), COLS)
            mixed_ref[n, r] = (x_ref[n, r].astype(F32) + ng[at, :]).astype(BF16)
        return 0

    lax.fori_loop(0, NIMG, mix_step, 0)

    def grad_step(r, _):
        total = None
        for dr in range(3):
            for dc in range(3):
                t = 3 * dr + dc
                part = lax.dot_general(
                    U3[pl.ds(al((r + 2 - dr) * PIX, 16), PIX), dc * CH : (dc + 1) * CH],
                    W[t * CH : (t + 1) * CH, :],
                    (((1,), (1,)), ((), ())),
                    preferred_element_type=F32,
                )
                total = part if total is None else total + part
        ng[pl.ds(al(r * PIX, 16), PIX), :] = total
        return 0

    lax.fori_loop(0, 2, grad_step, 0)

    def norm_step(n, _):
        first = jnp.zeros((1, CH), F32)
        second = jnp.zeros((1, CH), F32)
        for r in range(2):
            at = pl.ds(al(r * PIX + n * COLS, 32), COLS)
            cen = centred_of(x_ref[n, r].astype(F32), n)
            normed = cen * gain + bias
            sg = sigmoid(normed)
            grad = ng[at, :] * sg * (1.0 + normed * (1.0 - sg))
            ng[at, :] = grad
            first = first + jnp.sum(grad, axis=0, keepdims=True)
            second = second + jnp.sum(grad * cen, axis=0, keepdims=True)
        chs[0, pl.ds(n, 1), :] = first
        chs[1, pl.ds(n, 1), :] = second
        return 0

    lax.fori_loop(0, NIMG, norm_step, 0)
    bst_s[...] = to_groups(chs[0] * gain, chs[1] * gain)
    bst = (bst_s, bst_r, bst_ss, bst_rs)
    sp_start(*bst)
    row = lax.broadcasted_iota(jnp.int32, (8, CH), 0)
    gain_part = jnp.sum(chs[1], axis=0, keepdims=True)
    bias_part = jnp.sum(chs[0], axis=0, keepdims=True)
    gb_s[...] = jnp.where(row == 0, gain_part, jnp.where(row == 1, bias_part, 0.0))
    gbx = (gb_s, gb_r, gb_ss, gb_rs)
    sp_start(*gbx)

    def x2(g, k):
        to = lax.rem(x + k, 4)
        return rcopy(
            x2s.at[g, pl.ds(al(to * 160, 16), 160), :],
            x2r.at[g, k - 1],
            x2_ss.at[3 * g + k - 1],
            x2_rs.at[3 * g + k - 1],
            xdev(k),
        )

    def to_x(g, _):
        total = s1[pl.ds(3 * g, 3), z].astype(F32)
        for k in (1, 3, 2):
            zsum(g, k).wait_recv()
            total = total + r1[g, k - 1].astype(F32)
        flat = jnp.concatenate([total.reshape(240, CH), jnp.zeros((16, CH), F32)], axis=0)
        x2s[g] = flat.T.astype(BF16)
        for k in (1, 3, 2):
            x2(g, k).start()
        return 0

    lax.fori_loop(0, 3, to_x, 0)

    sp_wait(*gbx)
    gbt = slot_sum(gb_r)
    gb_s2 = gb2_r.at[dp]
    gb2_r[dp] = gbt

    def gb2(k):
        return rcopy(gb_s2, gb_s2, gb2_ss.at[k], gb2_rs.at[dp], (lax.rem(dp + k, 8), s))

    for k in range(1, 8):
        gb2(k).start()

    sp_wait(*bst)
    btot = slot_sum(bst_r)
    chs[0] = to_chans(btot, 0)
    chs[1] = to_chans(btot, 16)

    def in_step(n, _):
        for r in range(2):
            at = pl.ds(al(r * PIX + n * COLS, 32), COLS)
            cen = centred_of(x_ref[n, r].astype(F32), n)
            inner = ng[at, :] * gain - chs[0, pl.ds(n, 1), :] - cen * chs[1, pl.ds(n, 1), :]
            ig_ref[n, r] = (up_ref[n, r].astype(F32) + mcs[1, pl.ds(n, 1), :] * inner).astype(BF16)
        return 0

    lax.fori_loop(0, NIMG, in_step, 0)

    for g in range(3):
        total = x2s[g, pl.ds(al(x * 160, 16), 160), :].astype(F32)
        for k in (1, 3, 2):
            x2(g, k).wait_recv()
            total = total + x2r[g, k - 1].astype(F32)
        for j in range(4):
            y2s[j, :, g * 256 : (g + 1) * 256] = total[40 * j : 40 * (j + 1), :]

    def y2(j):
        return rcopy(y2s.at[j], y2r.at[y], y2_ss.at[j], y2_rs.at[y], (z * 2 + c, 4 * x + j))

    def y2_mine(j):
        return (c == ylo) & (4 * x + j == s)

    for j in range(4):
        @pl.when(jnp.logical_not(y2_mine(j)))
        def _():
            y2(j).start()

        @pl.when(y2_mine(j))
        def _():
            y2r[y] = y2s[j]

    for k in range(1, 8):
        slot = lax.rem(dp + k, 8)
        rcopy(gb_s2, gb2_r.at[slot], gb2_ss.at[k], gb2_rs.at[slot], (slot, s)).wait_recv()
    gb_ref[...] = slot_sum(gb2_r)

    for j in range(4):
        @pl.when(jnp.logical_not((c == ylo) & (y == j)))
        def _():
            rcopy(y2s.at[0], y2r.at[j], y2_ss.at[j], y2_rs.at[j], sib).wait_recv()

    wg_ref[...] = slot_sum(y2r)

    sp_drain(*st)
    for j in range(2):
        ag_y(j).wait_send()
        for k in range(1, 4):
            ag_z(k, j, False).wait_send()
            ag_z(k, j, True).wait_send()
    for i in range(4):
        halo(i).wait_send()
    for k in range(1, 4):
        ax(k).wait_send()
    for k in range(4):
        fw(k).wait_send()

    def sib_drain(t, _):
        sib_copy(t).wait_send()
        return 0

    lax.fori_loop(0, 9, sib_drain, 0)

    def sum_drain(g, _):
        for k in range(1, 4):
            zsum(g, k).wait_send()
            x2(g, k).wait_send()
        return 0

    lax.fori_loop(0, 3, sum_drain, 0)
    sp_drain(*bst)
    sp_drain(*gbx)
    for k in range(1, 8):
        gb2(k).wait_send()
    for j in range(4):
        @pl.when(jnp.logical_not(y2_mine(j)))
        def _():
            y2(j).wait_send()


def body(inputs, norm_gain, norm_bias, conv_weight, upstream):
    dma = pltpu.SemaphoreType.DMA
    vm = pltpu.VMEM
    scratch = [
        vm((2, NIMG, COLS, CH), BF16),
        vm((2, NIMG, COLS, CH), BF16),
        vm((4 * PIX, 3 * CH), BF16),
        vm((4 * PIX, 3 * CH), BF16),
        vm((2, 320, OWN), BF16),
        vm((9 * CH, CH), BF16),
        vm((9, 320, CH), BF16),
        vm((9, 320, CH), BF16),
        vm((9, 4, 80, CH), BF16),
        vm((3, 3, 3, 80, CH), BF16),
        vm((3, CH, 256), BF16),
        vm((3, 3, 160, 256), BF16),
        vm((4, 40, 768), F32),
        vm((4, 40, 768), F32),
        vm((OWN, CH), F32),
        vm((2, 16, CH), F32),
        vm((2, 16, CH), F32),
        vm((16, 128), F32),
        vm((16, 16, 128), F32),
        vm((16, 128), F32),
        vm((16, 16, 128), F32),
        vm((8, CH), F32),
        vm((16, 8, CH), F32),
        vm((8, 8, CH), F32),
        dma((16,)), dma((16,)),
        dma((16,)), dma((16,)),
        dma((16,)), dma((16,)),
        dma((8,)), dma((8,)),
        dma((4,)), dma((4,)),
        dma((14,)), dma((14,)),
        dma((3,)), dma((3,)),
        dma((4,)), dma((4,)),
        dma((9,)), dma((9,)),
        dma((9,)), dma((9,)),
        dma((9,)), dma((9,)),
        dma((4,)), dma((4,)),
    ]
    spec = pl.BlockSpec(memory_space=pltpu.VMEM)
    mixed, input_grad, wg, gb = pl.pallas_call(
        kernel,
        out_shape=(
            jax.ShapeDtypeStruct(inputs.shape, BF16),
            jax.ShapeDtypeStruct(inputs.shape, BF16),
            jax.ShapeDtypeStruct((40, 768), F32),
            jax.ShapeDtypeStruct((8, CH), F32),
        ),
        in_specs=[spec] * 5,
        out_specs=(spec,) * 4,
        scratch_shapes=scratch,
        compiler_params=pltpu.CompilerParams(
            collective_id=0, has_side_effects=True, vmem_limit_bytes=62 * 2**20
        ),
        name="resblock",
    )(inputs, norm_gain.reshape(1, CH), norm_bias.reshape(1, CH), conv_weight, upstream)
    wg = wg.reshape(40, 3, 256)[:, :, :240].reshape(40, 9, 80).transpose(1, 2, 0)
    return (mixed, input_grad, wg, gb[0], gb[1])


def solution(mesh):
    in_specs = (
        P("dp", "space", None, None),
        P(),
        P(),
        P(None, "dp", None),
        P("dp", "space", None, None),
    )
    out_specs = (
        P("dp", "space", None, None),
        P("dp", "space", None, None),
        P(None, "dp", "space"),
        P(),
        P(),
    )
    return jax.shard_map(body, mesh=mesh, in_specs=in_specs, out_specs=out_specs, check_vma=False)
```

```python
import functools

import jax
import jax.numpy as jnp
from jax import lax
from jax.experimental import pallas as pl
from jax.experimental.pallas import tpu as pltpu
from jax.sharding import PartitionSpec as P

GSIZE = 40
EPS = 1e-05
MESH = pl.DeviceIdType.MESH
NIMG = 14
COLS = 32
CH = 640
PIX = NIMG * COLS
OWN = 2 * PIX
COUNT = float(32 * 32 * GSIZE)
F32 = jnp.float32
BF16 = jnp.bfloat16
HIGH = lax.Precision.HIGHEST


def rcopy(src, dst, ssem, rsem, dev):
    return pltpu.make_async_remote_copy(
        src_ref=src, dst_ref=dst, send_sem=ssem, recv_sem=rsem, device_id=dev, device_id_type=MESH
    )


def al(value, unit):
    return pl.multiple_of(value, unit)


def sigmoid(v):
    return 1.0 / (1.0 + jnp.exp(-v))


def kernel(
    x_ref, gain_ref, bias_ref, w_ref, up_ref,
    mixed_ref, ig_ref, wg_ref, gg_ref, bg_ref,
    xh, uh, A3, U3, aT, W, sib_s, sib_r, s1, own1, wide, r1, x2s, x2r, y2s, y2r, ng,
    chs, mcs, st_s, st_r, bst_s, bst_r, gb_s, gb_r, gb2_r,
    st_ss, st_rs, bst_ss, bst_rs, gb_ss, gb_rs, gb2_ss, gb2_rs,
    h_ss, h_rs, ag_ss, ag_rs, ax_ss, ax_rs, fw_ss, fw_rs,
    sib_ss, sib_rs, z_ss, z_rs, x2_ss, x2_rs, y2_ss, y2_rs,
):
    dp = lax.axis_index("dp")
    s = lax.axis_index("space")
    x = lax.div(s, 4)
    yhi = lax.rem(lax.div(s, 2), 2)
    c = lax.rem(s, 2)
    z = lax.div(dp, 2)
    ylo = lax.rem(dp, 2)
    y = yhi * 2 + ylo
    sib = (dp, s + 1 - 2 * c)

    def zdev(k):
        return (lax.rem(z + k, 4) * 2 + ylo, s)

    def xdev(k):
        return (dp, lax.rem(s + 4 * k, 16))

    def ydev(k):
        to = lax.rem(y + k, 4)
        return (z * 2 + lax.rem(to, 2), (x * 2 + lax.div(to, 2)) * 2 + c)

    bar = pltpu.get_barrier_semaphore()

    def greet(dev):
        pl.semaphore_signal(bar, inc=1, device_id=dev, device_id_type=MESH)

    for k in range(1, 16):
        greet((dp, lax.rem(s + k, 16)))
    for k in range(1, 8):
        greet((lax.rem(dp + k, 8), s))
    for a, b in ((0, 1), (1, 0), (1, 1)):
        other = (x * 2 + lax.rem(yhi + a, 2)) * 2 + lax.rem(c + b, 2)
        greet((z * 2 + 1 - ylo, other))

    def table(shape, chan_dim, shift):
        chan = lax.broadcasted_iota(jnp.int32, shape, chan_dim)
        lane = lax.broadcasted_iota(jnp.int32, shape, 1 - chan_dim) - shift
        return jnp.where((chan >= lane * GSIZE) & (chan < (lane + 1) * GSIZE), 1.0, 0.0).astype(F32)

    def to_groups(first, second):
        return jnp.dot(first, table((CH, 128), 0, 0), precision=HIGH, preferred_element_type=F32) + jnp.dot(
            second, table((CH, 128), 0, 16), precision=HIGH, preferred_element_type=F32
        )

    def to_chans(vals, shift):
        return jnp.dot(vals, table((128, CH), 1, shift), precision=HIGH, preferred_element_type=F32) / COUNT

    chs[...] = jnp.zeros_like(chs)

    def stat_step(n, _):
        v = x_ref[n].astype(F32).reshape(2 * COLS, CH)
        chs[0, pl.ds(n, 1), :] = jnp.sum(v, axis=0, keepdims=True)
        chs[1, pl.ds(n, 1), :] = jnp.sum(v * v, axis=0, keepdims=True)
        return 0

    lax.fori_loop(0, NIMG, stat_step, 0)
    stats = to_groups(chs[0], chs[1])
    st_s[...] = stats
    tb = 8 * c + (4 + x) * (1 - c)
    ta = 2 * c
    W[tb, pl.ds(al(dp * 80, 16), 80), :] = w_ref[tb]
    W[pl.ds(ta, 2), pl.ds(al(dp * 80, 16), 80), :] = w_ref[pl.ds(ta, 2)]

    def put3(dst, row, n, v, flip):
        at = pl.ds(al(row * PIX + n * COLS, 32), COLS)
        col = lax.broadcasted_iota(jnp.int32, (COLS, CH), 0)
        prev = jnp.where(col == 0, 0.0, pltpu.roll(v, 1, 0))
        after = jnp.where(col == COLS - 1, 0.0, pltpu.roll(v, COLS - 1, 0))
        first, last = (after, prev) if flip else (prev, after)
        dst[at, 0:CH] = first.astype(BF16)
        dst[at, CH : 2 * CH] = v.astype(BF16)
        dst[at, 2 * CH : 3 * CH] = last.astype(BF16)

    def up_own(n, _):
        for r in range(2):
            put3(U3, r + 1, n, up_ref[n, r].astype(F32), True)
        return 0

    lax.fori_loop(0, NIMG, up_own, 0)
    pl.semaphore_wait(bar, 25)

    def sp_copy(src, dst, ssem, rsem, k):
        return rcopy(src, dst.at[s], ssem.at[k], rsem.at[s], (dp, lax.rem(s + k, 16)))

    def sp_start(src, dst, ssem, rsem):
        def step(k, _):
            sp_copy(src, dst, ssem, rsem, k).start()
            return 0

        lax.fori_loop(1, 16, step, 0)
        dst[s] = src[...]

    def sp_wait(src, dst, ssem, rsem):
        def step(k, _):
            slot = lax.rem(s + k, 16)
            rcopy(src, dst.at[slot], ssem.at[k], rsem.at[slot], (dp, slot)).wait_recv()
            return 0

        lax.fori_loop(1, 16, step, 0)

    def sp_drain(src, dst, ssem, rsem):
        def step(k, _):
            sp_copy(src, dst, ssem, rsem, k).wait_send()
            return 0

        lax.fori_loop(1, 16, step, 0)

    st = (st_s, st_r, st_ss, st_rs)
    sp_start(*st)

    def wsrc(j):
        return w_ref.at[pl.ds(tb, 1)] if j == 0 else w_ref.at[pl.ds(ta, 2)]

    def wrows(j, block):
        taps = pl.ds(tb, 1) if j == 0 else pl.ds(ta, 2)
        return W.at[taps, pl.ds(al(block * 80, 16), 80), :]

    ystep = ydev(1 + 2 * c)
    dpo = z * 2 + 1 - ylo

    def ag_y(j):
        return rcopy(wsrc(j), wrows(j, dp), ag_ss.at[j], ag_rs.at[j], ystep)

    def ag_z(k, j, relay):
        idx = 2 + 2 * (k - 1) + j + (6 if relay else 0)
        src = wrows(j, dpo) if relay else wsrc(j)
        return rcopy(src, wrows(j, dpo if relay else dp), ag_ss.at[idx], ag_rs.at[idx], zdev(k))

    def ag_y_recv(j):
        return rcopy(wsrc(j), wrows(j, dpo), ag_ss.at[j], ag_rs.at[j], ystep)

    def ag_z_recv(k, j, relay):
        idx = 2 + 2 * (k - 1) + j + (6 if relay else 0)
        block = lax.rem(z + 4 - k, 4) * 2 + (1 - ylo if relay else ylo)
        return rcopy(wsrc(j), wrows(j, block), ag_ss.at[idx], ag_rs.at[idx], zdev(k))

    def ax(k, m):
        rows = pl.ds(al(lax.rem(z + 4 - m, 4) * 160, 16), 160)
        i = 4 * (k - 1) + m
        return rcopy(W.at[4 + x, rows], W.at[4 + x, rows], ax_ss.at[i], ax_rs.at[i], xdev(k))

    def ax_recv(k, m):
        rows = pl.ds(al(lax.rem(z + 4 - m, 4) * 160, 16), 160)
        i = 4 * (k - 1) + m
        tap = 4 + lax.rem(x + 4 - k, 4)
        return rcopy(W.at[tap, rows], W.at[tap, rows], ax_ss.at[i], ax_rs.at[i], xdev(k))

    def ax_send(m):
        @pl.when(c == 0)
        def _():
            for k in (1, 3, 2):
                ax(k, m).start()

    def fw_a(far):
        taps = pl.ds(2 - ta if far else ta, 2)
        return rcopy(W.at[taps], W.at[taps], fw_ss.at[0], fw_rs.at[0], sib)

    def fw_b(tap, i):
        return rcopy(W.at[tap], W.at[tap], fw_ss.at[i], fw_rs.at[i], sib)

    for j in range(2):
        ag_y(j).start()

    above = (dp, lax.rem(s + 15, 16))
    below = (dp, lax.rem(s + 1, 16))

    def halo(i):
        ref, dst = (up_ref, uh) if i < 2 else (x_ref, xh)
        if i % 2 == 0:
            return rcopy(ref.at[:, 0], dst.at[1], h_ss.at[i], h_rs.at[i], above)
        return rcopy(ref.at[:, 1], dst.at[0], h_ss.at[i], h_rs.at[i], below)

    for i in range(2):
        halo(i).start()
    for j in range(2):
        for k in (1, 3, 2):
            ag_z(k, j, False).start()


    for j in range(2):
        ag_y_recv(j).wait_recv()
        for k in (1, 3, 2):
            ag_z(k, j, True).start()
        if j == 0:
            ax_send(0)
    for i in range(2, 4):
        halo(i).start()

    sp_wait(*st)

    def slot_sum(ref):
        total = ref[0]
        for i in range(1, ref.shape[0]):
            total = total + ref[i]
        return total

    tot = slot_sum(st_r)
    mean = to_chans(tot, 0)
    mcs[0] = mean
    mcs[1] = lax.rsqrt(to_chans(tot, 16) - mean * mean + EPS)
    gain = gain_ref[...].reshape(1, CH)
    bias = bias_ref[...].reshape(1, CH)

    def centred_of(v, n):
        return (v - mcs[0, pl.ds(n, 1), :]) * mcs[1, pl.ds(n, 1), :]

    def act_of(v, n):
        normed = centred_of(v, n) * gain + bias
        return normed * sigmoid(normed)

    def act_own(n, _):
        for r in range(2):
            put3(A3, r + 1, n, act_of(x_ref[n, r].astype(F32), n), False)
        return 0

    lax.fori_loop(0, NIMG, act_own, 0)

    def turn(m, _):
        block = A3[pl.ds(al(PIX + m * 128, 16), 128), CH : 2 * CH].astype(F32).T.astype(BF16)
        for q in range(4):
            for p in range(2):
                d = 2 * q + p
                aT[p, q * 80 : (q + 1) * 80, pl.ds(al(m * 128, 128), 128)] = block[d * 80 : (d + 1) * 80]
        return 0

    lax.fori_loop(0, OWN // 128, turn, 0)

    for k in (1, 3, 2):
        ag_z_recv(k, 0, False).wait_recv()
        ag_z_recv(k, 0, True).wait_recv()
        ax_send(k)
    fw_b(tb, 1).start()

    for i in range(2):
        halo(i).wait_recv()

    def masked(v, edge):
        return jnp.where(s == (0 if edge == 0 else 15), jnp.zeros_like(v), v)

    def up_halo(n, _):
        for e in range(2):
            put3(U3, 3 * e, n, masked(uh[e, n].astype(F32), e), True)
        return 0

    lax.fori_loop(0, NIMG, up_halo, 0)

    def terms(p, dr, dc):
        rhs = U3[pl.ds(al((2 - dr) * PIX, 16), OWN), dc * CH : (dc + 1) * CH]
        return jnp.dot(aT[p], rhs, preferred_element_type=F32)

    def sib_copy(t):
        return rcopy(sib_s.at[t], sib_r.at[t], sib_ss.at[t], sib_rs.at[t], sib)

    def far_step(dr, _):
        for dc in range(3):
            t = 3 * dr + dc
            sib_s[t] = terms(1 - c, dr, dc).astype(BF16)
            sib_copy(t).start()
        return 0

    lax.fori_loop(0, 3, far_step, 0)
    for k in (1, 3, 2):
        ag_z_recv(k, 1, False).wait_recv()
        ag_z_recv(k, 1, True).wait_recv()
    fw_a(False).start()

    axes = ((zdev, xdev), (xdev, ydev), (ydev, zdev))
    order = ((z, x, y), (x, y, z), (y, z, x))

    def sum1(g, k):
        i = 3 * g + k - 1
        to = lax.rem(order[g][0] + k, 4)
        return rcopy(s1.at[pl.ds(3 * g, 3), to], r1.at[g, k - 1], z_ss.at[i], z_rs.at[i], axes[g][0](k))

    for dr in range(3):
        for dc in range(3):
            t = 3 * dr + dc
            near = terms(c, dr, dc)
            sib_copy(t).wait_recv()
            near = (near + sib_r[t].astype(F32)).reshape(4, 80, CH)
            s1[t] = near.astype(BF16)
            wide[...] = near
            own1[t] = wide[order[dr][0]]
        for k in (1, 3, 2):
            sum1(dr, k).start()

    @pl.when(c == 0)
    def _():
        for k in (1, 3, 2):
            for m in range(4):
                ax_recv(k, m).wait_recv()
            fw_b(4 + lax.rem(x + 4 - k, 4), 1 + k).start()
        fw_b(8, 1).wait_recv()

    @pl.when(c == 1)
    def _():
        fw_b(4 + x, 1).wait_recv()
        for k in (1, 3, 2):
            fw_b(4 + lax.rem(x + 4 - k, 4), 1 + k).wait_recv()

    fw_a(True).wait_recv()

    def grad_step(r, _):
        total = None
        for dr in range(3):
            for dc in range(3):
                t = 3 * dr + dc
                part = lax.dot_general(
                    U3[pl.ds(al((r + 2 - dr) * PIX, 16), PIX), dc * CH : (dc + 1) * CH],
                    W[t],
                    (((1,), (1,)), ((), ())),
                    preferred_element_type=F32,
                )
                total = part if total is None else total + part
        ng[pl.ds(al(r * PIX, 16), PIX), :] = total
        return 0

    lax.fori_loop(0, 2, grad_step, 0)

    def norm_step(n, _):
        first = jnp.zeros((1, CH), F32)
        second = jnp.zeros((1, CH), F32)
        for r in range(2):
            at = pl.ds(al(r * PIX + n * COLS, 32), COLS)
            cen = centred_of(x_ref[n, r].astype(F32), n)
            normed = cen * gain + bias
            sg = sigmoid(normed)
            grad = ng[at, :] * sg * (1.0 + normed * (1.0 - sg))
            ng[at, :] = grad
            first = first + jnp.sum(grad, axis=0, keepdims=True)
            second = second + jnp.sum(grad * cen, axis=0, keepdims=True)
        chs[0, pl.ds(n, 1), :] = first
        chs[1, pl.ds(n, 1), :] = second
        return 0

    lax.fori_loop(0, NIMG, norm_step, 0)
    bst_s[...] = to_groups(chs[0] * gain, chs[1] * gain)
    bst = (bst_s, bst_r, bst_ss, bst_rs)
    sp_start(*bst)
    row = lax.broadcasted_iota(jnp.int32, (8, CH), 0)
    gain_part = jnp.sum(chs[1], axis=0, keepdims=True)
    bias_part = jnp.sum(chs[0], axis=0, keepdims=True)
    gb_s[...] = jnp.where(row == 0, gain_part, jnp.where(row == 1, bias_part, 0.0))
    gbx = (gb_s, gb_r, gb_ss, gb_rs)
    sp_start(*gbx)

    def sum2(g, k):
        i = 3 * g + k - 1
        rows = pl.ds(al(lax.rem(order[g][1] + k, 4) * 160, 16), 160)
        return rcopy(x2s.at[g, rows, :], x2r.at[g, k - 1], x2_ss.at[i], x2_rs.at[i], axes[g][1](k))

    for g in range(3):
        total = own1[3 * g : 3 * g + 3]
        for k in (1, 3, 2):
            sum1(g, k).wait_recv()
            total = total + r1[g, k - 1].astype(F32)
        x2s[g] = jnp.concatenate([total.reshape(240, CH), jnp.zeros((16, CH), F32)], axis=0).T
        for k in (1, 3, 2):
            sum2(g, k).start()

    for i in range(2, 4):
        halo(i).wait_recv()

    def act_halo(n, _):
        for e in range(2):
            put3(A3, 3 * e, n, masked(act_of(xh[e, n].astype(F32), n), e), False)
        return 0

    lax.fori_loop(0, NIMG, act_halo, 0)

    def conv_step(r, _):
        total = None
        for dr in range(3):
            part = jnp.dot(
                A3[pl.ds(al((r + dr) * PIX, 16), PIX), :],
                W[3 * dr : 3 * dr + 3].reshape(3 * CH, CH),
                preferred_element_type=F32,
            )
            total = part if total is None else total + part
        mixed_ref[:, r] = (x_ref[:, r].astype(F32) + total.reshape(NIMG, COLS, CH)).astype(BF16)
        return 0

    lax.fori_loop(0, 2, conv_step, 0)

    def sum3(g, j):
        i = 4 * g + j
        return rcopy(
            y2s.at[g, j], y2r.at[g, order[g][2]], y2_ss.at[i], y2_rs.at[4 * g + order[g][2]],
            (order[g][0] * 2 + c, order[g][1] * 4 + j),
        )

    def sum3_mine(g, j):
        return (order[g][0] * 2 + c == dp) & (order[g][1] * 4 + j == s)

    for g in range(3):
        total = x2s[g, pl.ds(al(order[g][1] * 160, 16), 160), :]
        for k in (1, 3, 2):
            sum2(g, k).wait_recv()
            total = total + x2r[g, k - 1]
        for j in range(4):
            y2s[g, j] = total[40 * j : 40 * (j + 1), :]
        for j in range(4):
            @pl.when(jnp.logical_not(sum3_mine(g, j)))
            def _():
                sum3(g, j).start()

            @pl.when(sum3_mine(g, j))
            def _():
                y2r[g, order[g][2]] = y2s[g, j]

    sp_wait(*gbx)
    gbt = slot_sum(gb_r)
    gb_s2 = gb2_r.at[dp]
    gb2_r[dp] = gbt

    def gb2(k):
        return rcopy(gb_s2, gb_s2, gb2_ss.at[k], gb2_rs.at[dp], (lax.rem(dp + k, 8), s))

    for k in range(1, 8):
        gb2(k).start()

    sp_wait(*bst)
    btot = slot_sum(bst_r)
    chs[0] = to_chans(btot, 0)
    chs[1] = to_chans(btot, 16)

    def in_step(n, _):
        for r in range(2):
            at = pl.ds(al(r * PIX + n * COLS, 32), COLS)
            cen = centred_of(x_ref[n, r].astype(F32), n)
            inner = ng[at, :] * gain - chs[0, pl.ds(n, 1), :] - cen * chs[1, pl.ds(n, 1), :]
            ig_ref[n, r] = (up_ref[n, r].astype(F32) + mcs[1, pl.ds(n, 1), :] * inner).astype(BF16)
        return 0

    lax.fori_loop(0, NIMG, in_step, 0)

    for k in range(1, 8):
        slot = lax.rem(dp + k, 8)
        rcopy(gb_s2, gb2_r.at[slot], gb2_ss.at[k], gb2_rs.at[slot], (slot, s)).wait_recv()
    totals = slot_sum(gb2_r)
    gg_ref[...] = totals[0:1].reshape(CH)
    bg_ref[...] = totals[1:2].reshape(CH)

    def from_me(g, i):
        p1, p2, p3 = order[g]
        return (p1 == z) & (p2 == x) & (p3 == i) & (c == ylo)

    for g in range(3):
        for i in range(4):
            @pl.when(jnp.logical_not(from_me(g, i)))
            def _():
                rcopy(y2s.at[g, 0], y2r.at[g, i], y2_ss.at[4 * g], y2_rs.at[4 * g + i], sib).wait_recv()

        total = slot_sum(y2r[g])
        for dc in range(3):
            wg_ref[3 * g + dc] = total[:, 80 * dc : 80 * (dc + 1)]

    sp_drain(*st)
    for j in range(2):
        ag_y(j).wait_send()
        for k in range(1, 4):
            ag_z(k, j, False).wait_send()
            ag_z(k, j, True).wait_send()
    for i in range(4):
        halo(i).wait_send()
    fw_a(False).wait_send()
    fw_b(tb, 1).wait_send()

    @pl.when(c == 0)
    def _():
        for k in range(1, 4):
            for m in range(4):
                ax(k, m).wait_send()
            fw_b(4 + x, 1 + k).wait_send()


    def sib_drain(t, _):
        sib_copy(t).wait_send()
        return 0

    lax.fori_loop(0, 9, sib_drain, 0)

    for g in range(3):
        for k in range(1, 4):
            sum1(g, k).wait_send()
            sum2(g, k).wait_send()
    sp_drain(*bst)
    sp_drain(*gbx)
    for k in range(1, 8):
        gb2(k).wait_send()
    for g in range(3):
        for j in range(4):
            @pl.when(jnp.logical_not(sum3_mine(g, j)))
            def _():
                sum3(g, j).wait_send()


def body(inputs, norm_gain, norm_bias, conv_weight, upstream):
    dma = pltpu.SemaphoreType.DMA
    vm = pltpu.VMEM
    scratch = [
        vm((2, NIMG, COLS, CH), BF16),
        vm((2, NIMG, COLS, CH), BF16),
        vm((4 * PIX, 3 * CH), BF16),
        vm((4 * PIX, 3 * CH), BF16),
        vm((2, 320, OWN), BF16),
        vm((9, CH, CH), BF16),
        vm((9, 320, CH), BF16),
        vm((9, 320, CH), BF16),
        vm((9, 4, 80, CH), BF16),
        vm((9, 80, CH), F32),
        vm((4, 80, CH), F32),
        vm((3, 3, 3, 80, CH), BF16),
        vm((3, CH, 256), F32),
        vm((3, 3, 160, 256), F32),
        vm((3, 4, 40, 256), F32),
        vm((3, 4, 40, 256), F32),
        vm((OWN, CH), F32),
        vm((2, 16, CH), F32),
        vm((2, 16, CH), F32),
        vm((16, 128), F32),
        vm((16, 16, 128), F32),
        vm((16, 128), F32),
        vm((16, 16, 128), F32),
        vm((8, CH), F32),
        vm((16, 8, CH), F32),
        vm((8, 8, CH), F32),
        dma((16,)), dma((16,)),
        dma((16,)), dma((16,)),
        dma((16,)), dma((16,)),
        dma((8,)), dma((8,)),
        dma((4,)), dma((4,)),
        dma((14,)), dma((14,)),
        dma((12,)), dma((12,)),
        dma((5,)), dma((5,)),
        dma((9,)), dma((9,)),
        dma((9,)), dma((9,)),
        dma((9,)), dma((9,)),
        dma((12,)), dma((12,)),
    ]
    spec = pl.BlockSpec(memory_space=pltpu.VMEM)
    mixed, input_grad, wg, gain_grad, bias_grad = pl.pallas_call(
        kernel,
        out_shape=(
            jax.ShapeDtypeStruct(inputs.shape, BF16),
            jax.ShapeDtypeStruct(inputs.shape, BF16),
            jax.ShapeDtypeStruct((9, 40, 80), F32),
            jax.ShapeDtypeStruct((CH,), F32),
            jax.ShapeDtypeStruct((CH,), F32),
        ),
        in_specs=[spec] * 5,
        out_specs=(spec,) * 5,
        scratch_shapes=scratch,
        compiler_params=pltpu.CompilerParams(
            collective_id=0, has_side_effects=True, vmem_limit_bytes=62 * 2**20
        ),
        name="resblock",
    )(inputs, norm_gain, norm_bias, conv_weight, upstream)
    return (mixed, input_grad, wg.transpose(0, 2, 1), gain_grad, bias_grad)


def solution(mesh):
    in_specs = (
        P("dp", "space", None, None),
        P(),
        P(),
        P(None, "dp", None),
        P("dp", "space", None, None),
    )
    out_specs = (
        P("dp", "space", None, None),
        P("dp", "space", None, None),
        P(None, "dp", "space"),
        P(),
        P(),
    )
    return jax.shard_map(body, mesh=mesh, in_specs=in_specs, out_specs=out_specs, check_vma=False)
```

```python
import functools

import jax
import jax.numpy as jnp
from jax import lax
from jax.experimental import pallas as pl
from jax.experimental.pallas import tpu as pltpu
from jax.sharding import PartitionSpec as P

GSIZE = 40
EPS = 1e-05
MESH = pl.DeviceIdType.MESH
NIMG = 14
COLS = 32
CH = 640
PIX = NIMG * COLS
OWN = 2 * PIX
COUNT = float(32 * 32 * GSIZE)
F32 = jnp.float32
BF16 = jnp.bfloat16
HIGH = lax.Precision.HIGHEST


def rcopy(src, dst, ssem, rsem, dev):
    return pltpu.make_async_remote_copy(
        src_ref=src, dst_ref=dst, send_sem=ssem, recv_sem=rsem, device_id=dev, device_id_type=MESH
    )


def al(value, unit):
    return pl.multiple_of(value, unit)


def sigmoid(v):
    return 1.0 / (1.0 + jnp.exp(-v))


def kernel(
    x_ref, gain_ref, bias_ref, w_ref, up_ref,
    mixed_ref, ig_ref, wg_ref, gg_ref, bg_ref,
    xh, uh, A3, U3, aT, W, sib_s, sib_r, s1, own1, wide, r1, x2s, x2r, wide2, own2, y2s, y2r, ng,
    chs, mcs, st_s, st_r, bst_s, bst_r, gb2_r,
    st_ss, st_rs, bst_ss, bst_rs, gb2_ss, gb2_rs,
    h_ss, h_rs, ag_ss, ag_rs, ax_ss, ax_rs, fw_ss, fw_rs,
    sib_ss, sib_rs, z_ss, z_rs, x2_ss, x2_rs, y2_ss, y2_rs,
):
    dp = lax.axis_index("dp")
    s = lax.axis_index("space")
    x = lax.div(s, 4)
    yhi = lax.rem(lax.div(s, 2), 2)
    c = lax.rem(s, 2)
    z = lax.div(dp, 2)
    ylo = lax.rem(dp, 2)
    y = yhi * 2 + ylo
    sib = (dp, s + 1 - 2 * c)

    def zdev(k):
        return (lax.rem(z + k, 4) * 2 + ylo, s)

    def xdev(k):
        return (dp, lax.rem(s + 4 * k, 16))

    def ydev(k):
        to = lax.rem(y + k, 4)
        return (z * 2 + lax.rem(to, 2), (x * 2 + lax.div(to, 2)) * 2 + c)

    bar = pltpu.get_barrier_semaphore()

    def greet(dev):
        pl.semaphore_signal(bar, inc=1, device_id=dev, device_id_type=MESH)

    for k in range(1, 16):
        greet((dp, lax.rem(s + k, 16)))
    for k in range(1, 8):
        greet((lax.rem(dp + k, 8), s))
    for a, b in ((0, 1), (1, 0), (1, 1)):
        other = (x * 2 + lax.rem(yhi + a, 2)) * 2 + lax.rem(c + b, 2)
        greet((z * 2 + 1 - ylo, other))

    def table(shape, chan_dim, shift):
        chan = lax.broadcasted_iota(jnp.int32, shape, chan_dim)
        lane = lax.broadcasted_iota(jnp.int32, shape, 1 - chan_dim) - shift
        return jnp.where((chan >= lane * GSIZE) & (chan < (lane + 1) * GSIZE), 1.0, 0.0).astype(F32)

    def to_groups(first, second):
        return jnp.dot(first, table((CH, 128), 0, 0), precision=HIGH, preferred_element_type=F32) + jnp.dot(
            second, table((CH, 128), 0, 16), precision=HIGH, preferred_element_type=F32
        )

    def to_chans(vals, shift):
        return jnp.dot(vals, table((128, CH), 1, shift), precision=HIGH, preferred_element_type=F32) / COUNT

    chs[...] = jnp.zeros_like(chs)

    def stat_step(n, _):
        v = x_ref[n].astype(F32).reshape(2 * COLS, CH)
        chs[0, pl.ds(n, 1), :] = jnp.sum(v, axis=0, keepdims=True)
        chs[1, pl.ds(n, 1), :] = jnp.sum(v * v, axis=0, keepdims=True)
        return 0

    lax.fori_loop(0, NIMG, stat_step, 0)
    stats = to_groups(chs[0], chs[1])
    st_s[...] = stats
    tb = 8 * c + (4 + x) * (1 - c)
    ta = 2 * c
    W[tb, pl.ds(al(dp * 80, 16), 80), :] = w_ref[tb]
    W[pl.ds(ta, 2), pl.ds(al(dp * 80, 16), 80), :] = w_ref[pl.ds(ta, 2)]

    def put3(dst, row, n, v, flip):
        at = pl.ds(al(row * PIX + n * COLS, 32), COLS)
        col = lax.broadcasted_iota(jnp.int32, (COLS, CH), 0)
        prev = jnp.where(col == 0, 0.0, pltpu.roll(v, 1, 0))
        after = jnp.where(col == COLS - 1, 0.0, pltpu.roll(v, COLS - 1, 0))
        first, last = (after, prev) if flip else (prev, after)
        dst[at, 0:CH] = first.astype(BF16)
        dst[at, CH : 2 * CH] = v.astype(BF16)
        dst[at, 2 * CH : 3 * CH] = last.astype(BF16)

    def up_own(n, _):
        for r in range(2):
            put3(U3, r + 1, n, up_ref[n, r].astype(F32), True)
        return 0

    lax.fori_loop(0, NIMG, up_own, 0)
    pl.semaphore_wait(bar, 25)

    def sp_start(src, dst, ssem, rsem):
        def step(k, _):
            rcopy(src, dst.at[s], ssem.at[0], rsem.at[0], (dp, lax.rem(s + k, 16))).start()
            return 0

        lax.fori_loop(1, 16, step, 0)
        dst[s] = src[...]

    def sp_wait(src, dst, ssem, rsem):
        most = dst.at[pl.ds(0, 15)]
        rcopy(most, most, ssem.at[0], rsem.at[0], sib).wait_recv()

    def sp_drain(src, dst, ssem, rsem):
        most = dst.at[pl.ds(0, 15)]
        rcopy(most, most, ssem.at[0], rsem.at[0], sib).wait_send()

    st = (st_s, st_r, st_ss, st_rs)
    sp_start(*st)

    def wsrc(j):
        return w_ref.at[pl.ds(tb, 1)] if j == 0 else w_ref.at[pl.ds(ta, 2)]

    def wrows(j, block):
        taps = pl.ds(tb, 1) if j == 0 else pl.ds(ta, 2)
        return W.at[taps, pl.ds(al(block * 80, 16), 80), :]

    ystep = ydev(1 + 2 * c)
    dpo = z * 2 + 1 - ylo

    def ag_y(j):
        return rcopy(wsrc(j), wrows(j, dp), ag_ss.at[j], ag_rs.at[j], ystep)

    def ag_z(k, j, relay):
        idx = 2 + 2 * (k - 1) + j + (6 if relay else 0)
        src = wrows(j, dpo) if relay else wsrc(j)
        return rcopy(src, wrows(j, dpo if relay else dp), ag_ss.at[idx], ag_rs.at[idx], zdev(k))

    def ag_y_recv(j):
        return rcopy(wsrc(j), wrows(j, dpo), ag_ss.at[j], ag_rs.at[j], ystep)

    def ag_z_recv(k, j, relay):
        idx = 2 + 2 * (k - 1) + j + (6 if relay else 0)
        block = lax.rem(z + 4 - k, 4) * 2 + (1 - ylo if relay else ylo)
        return rcopy(wsrc(j), wrows(j, block), ag_ss.at[idx], ag_rs.at[idx], zdev(k))

    def ax(k, m):
        rows = pl.ds(al(lax.rem(z + 4 - m, 4) * 160, 16), 160)
        i = 4 * (k - 1) + m
        return rcopy(W.at[4 + x, rows], W.at[4 + x, rows], ax_ss.at[i], ax_rs.at[i], xdev(k))

    def ax_recv(k, m):
        rows = pl.ds(al(lax.rem(z + 4 - m, 4) * 160, 16), 160)
        i = 4 * (k - 1) + m
        tap = 4 + lax.rem(x + 4 - k, 4)
        return rcopy(W.at[tap, rows], W.at[tap, rows], ax_ss.at[i], ax_rs.at[i], xdev(k))

    def ax_send(m):
        @pl.when(c == 0)
        def _():
            for k in (1, 3, 2):
                ax(k, m).start()

    def fw_a(far):
        taps = pl.ds(2 - ta if far else ta, 2)
        return rcopy(W.at[taps], W.at[taps], fw_ss.at[0], fw_rs.at[0], sib)

    def fw_b(tap, i):
        return rcopy(W.at[tap], W.at[tap], fw_ss.at[i], fw_rs.at[i], sib)

    for j in range(2):
        ag_y(j).start()

    above = (dp, lax.rem(s + 15, 16))
    below = (dp, lax.rem(s + 1, 16))

    def halo(i):
        ref, dst = (up_ref, uh) if i < 2 else (x_ref, xh)
        if i % 2 == 0:
            return rcopy(ref.at[:, 0], dst.at[1], h_ss.at[i], h_rs.at[i], above)
        return rcopy(ref.at[:, 1], dst.at[0], h_ss.at[i], h_rs.at[i], below)

    for i in range(2):
        halo(i).start()
    for j in range(2):
        for k in (1, 3, 2):
            ag_z(k, j, False).start()


    for j in range(2):
        ag_y_recv(j).wait_recv()
        for k in (1, 3, 2):
            ag_z(k, j, True).start()
        if j == 0:
            ax_send(0)

    sp_wait(*st)

    def slot_sum(ref):
        total = ref[0]
        for i in range(1, ref.shape[0]):
            total = total + ref[i]
        return total

    tot = slot_sum(st_r)
    mean = to_chans(tot, 0)
    mcs[0] = mean
    mcs[1] = lax.rsqrt(to_chans(tot, 16) - mean * mean + EPS)
    gain = gain_ref[...].reshape(1, CH)
    bias = bias_ref[...].reshape(1, CH)

    def centred_of(v, n):
        return (v - mcs[0, pl.ds(n, 1), :]) * mcs[1, pl.ds(n, 1), :]

    def act_of(v, n):
        normed = centred_of(v, n) * gain + bias
        return normed * sigmoid(normed)

    def act_own(n, _):
        for r in range(2):
            put3(A3, r + 1, n, act_of(x_ref[n, r].astype(F32), n), False)
        return 0

    lax.fori_loop(0, NIMG, act_own, 0)

    def turn(m, _):
        block = A3[pl.ds(al(PIX + m * 128, 16), 128), CH : 2 * CH].astype(F32).T.astype(BF16)
        for q in range(4):
            for p in range(2):
                d = 2 * q + p
                aT[p, q * 80 : (q + 1) * 80, pl.ds(al(m * 128, 128), 128)] = block[d * 80 : (d + 1) * 80]
        return 0

    lax.fori_loop(0, OWN // 128, turn, 0)

    for k in (1, 3, 2):
        ag_z_recv(k, 0, False).wait_recv()
        ag_z_recv(k, 0, True).wait_recv()
        ax_send(k)
    fw_b(tb, 1).start()

    for i in range(2):
        halo(i).wait_recv()

    def masked(v, edge):
        return jnp.where(s == (0 if edge == 0 else 15), jnp.zeros_like(v), v)

    def up_halo(n, _):
        for e in range(2):
            put3(U3, 3 * e, n, masked(uh[e, n].astype(F32), e), True)
        return 0

    for i in range(2, 4):
        halo(i).start()
    lax.fori_loop(0, NIMG, up_halo, 0)

    def terms(p, dr, dc):
        rhs = U3[pl.ds(al((2 - dr) * PIX, 16), OWN), dc * CH : (dc + 1) * CH]
        return jnp.dot(aT[p], rhs, preferred_element_type=F32)

    def sib_copy(t):
        return rcopy(sib_s.at[t], sib_r.at[t], sib_ss.at[t], sib_rs.at[t], sib)

    def far_step(dr, _):
        for dc in range(3):
            t = 3 * dr + dc
            sib_s[t] = terms(1 - c, dr, dc).astype(BF16)
            sib_copy(t).start()
        return 0

    lax.fori_loop(0, 3, far_step, 0)

    axes = ((zdev, xdev), (xdev, ydev), (ydev, zdev))
    order = ((z, x, y), (x, y, z), (y, z, x))

    def sum1(g, k):
        i = 3 * g + k - 1
        to = lax.rem(order[g][0] + k, 4)
        return rcopy(s1.at[pl.ds(3 * g, 3), to], r1.at[g, k - 1], z_ss.at[i], z_rs.at[i], axes[g][0](k))

    for dr in range(3):
        for dc in range(3):
            t = 3 * dr + dc
            near = terms(c, dr, dc)
            sib_copy(t).wait_recv()
            near = (near + sib_r[t].astype(F32)).reshape(4, 80, CH)
            s1[t] = near.astype(BF16)
            wide[...] = near
            own1[t] = wide[order[dr][0]]
        for k in (1, 3, 2):
            sum1(dr, k).start()

    for k in (1, 3, 2):
        ag_z_recv(k, 1, False).wait_recv()
        ag_z_recv(k, 1, True).wait_recv()
    fw_a(False).start()

    @pl.when(c == 0)
    def _():
        for k in (1, 3, 2):
            for m in range(4):
                ax_recv(k, m).wait_recv()
            fw_b(4 + lax.rem(x + 4 - k, 4), 1 + k).start()
        fw_b(8, 1).wait_recv()

    @pl.when(c == 1)
    def _():
        fw_b(4 + x, 1).wait_recv()
        for k in (1, 3, 2):
            fw_b(4 + lax.rem(x + 4 - k, 4), 1 + k).wait_recv()

    fw_a(True).wait_recv()

    def grad_step(r, _):
        total = None
        for dr in range(3):
            for dc in range(3):
                t = 3 * dr + dc
                part = lax.dot_general(
                    U3[pl.ds(al((r + 2 - dr) * PIX, 16), PIX), dc * CH : (dc + 1) * CH],
                    W[t],
                    (((1,), (1,)), ((), ())),
                    preferred_element_type=F32,
                )
                total = part if total is None else total + part
        ng[pl.ds(al(r * PIX, 16), PIX), :] = total
        return 0

    lax.fori_loop(0, 2, grad_step, 0)

    def norm_step(n, _):
        first = jnp.zeros((1, CH), F32)
        second = jnp.zeros((1, CH), F32)
        for r in range(2):
            at = pl.ds(al(r * PIX + n * COLS, 32), COLS)
            cen = centred_of(x_ref[n, r].astype(F32), n)
            normed = cen * gain + bias
            sg = sigmoid(normed)
            grad = ng[at, :] * sg * (1.0 + normed * (1.0 - sg))
            ng[at, :] = grad
            first = first + jnp.sum(grad, axis=0, keepdims=True)
            second = second + jnp.sum(grad * cen, axis=0, keepdims=True)
        chs[0, pl.ds(n, 1), :] = first
        chs[1, pl.ds(n, 1), :] = second
        return 0

    lax.fori_loop(0, NIMG, norm_step, 0)
    bst_s[0:16] = to_groups(chs[0] * gain, chs[1] * gain)
    for i in range(2):
        part = jnp.sum(chs[1 - i], axis=0, keepdims=True)
        for j in range(5):
            bst_s[16 + 5 * i + j : 17 + 5 * i + j] = part[:, 128 * j : 128 * (j + 1)]
    bst_s[26:32] = jnp.zeros((6, 128), F32)
    bst = (bst_s, bst_r, bst_ss, bst_rs)
    sp_start(*bst)

    def sum2(g, k):
        i = 3 * g + k - 1
        rows = pl.ds(al(lax.rem(order[g][1] + k, 4) * 160, 16), 160)
        return rcopy(x2s.at[g, rows, :], x2r.at[g, k - 1], x2_ss.at[i], x2_rs.at[i], axes[g][1](k))

    for g in range(3):
        total = own1[3 * g : 3 * g + 3]
        for k in (1, 3, 2):
            sum1(g, k).wait_recv()
            total = total + r1[g, k - 1].astype(F32)
        total = jnp.concatenate([total.reshape(240, CH), jnp.zeros((16, CH), F32)], axis=0).T
        wide2[...] = total
        own2[g] = wide2[pl.ds(al(order[g][1] * 160, 16), 160), :]
        x2s[g] = total.astype(BF16)
        for k in (1, 3, 2):
            sum2(g, k).start()

    for i in range(2, 4):
        halo(i).wait_recv()

    def act_halo(n, _):
        for e in range(2):
            put3(A3, 3 * e, n, masked(act_of(xh[e, n].astype(F32), n), e), False)
        return 0

    lax.fori_loop(0, NIMG, act_halo, 0)

    def conv_step(r, _):
        total = None
        for dr in range(3):
            part = jnp.dot(
                A3[pl.ds(al((r + dr) * PIX, 16), PIX), :],
                W[3 * dr : 3 * dr + 3].reshape(3 * CH, CH),
                preferred_element_type=F32,
            )
            total = part if total is None else total + part
        mixed_ref[:, r] = (x_ref[:, r].astype(F32) + total.reshape(NIMG, COLS, CH)).astype(BF16)
        return 0

    conv_step(0, 0)

    def sum3(g, j):
        i = 4 * g + j
        return rcopy(
            y2s.at[g, j], y2r.at[g, order[g][2]], y2_ss.at[i], y2_rs.at[4 * g + order[g][2]],
            (order[g][0] * 2 + c, order[g][1] * 4 + j),
        )

    def sum3_mine(g, j):
        return (order[g][0] * 2 + c == dp) & (order[g][1] * 4 + j == s)

    for g in range(3):
        total = own2[g]
        for k in (1, 3, 2):
            sum2(g, k).wait_recv()
            total = total + x2r[g, k - 1].astype(F32)
        for j in range(4):
            y2s[g, j] = total[40 * j : 40 * (j + 1), :]
        for j in range(4):
            @pl.when(jnp.logical_not(sum3_mine(g, j)))
            def _():
                sum3(g, j).start()

            @pl.when(sum3_mine(g, j))
            def _():
                y2r[g, order[g][2]] = y2s[g, j]

    conv_step(1, 0)

    sp_drain(*st)
    for j in range(2):
        ag_y(j).wait_send()
        for k in range(1, 4):
            ag_z(k, j, False).wait_send()
            ag_z(k, j, True).wait_send()
    for i in range(4):
        halo(i).wait_send()
    fw_a(False).wait_send()
    fw_b(tb, 1).wait_send()

    @pl.when(c == 0)
    def _():
        for k in range(1, 4):
            for m in range(4):
                ax(k, m).wait_send()
            fw_b(4 + x, 1 + k).wait_send()


    def sib_drain(t, _):
        sib_copy(t).wait_send()
        return 0

    lax.fori_loop(0, 9, sib_drain, 0)

    for g in range(3):
        for k in range(1, 4):
            sum1(g, k).wait_send()
            sum2(g, k).wait_send()

    sp_wait(*bst)
    btot = slot_sum(bst_r)
    gb2_r[dp] = btot[16:32]
    gb_own = gb2_r.at[dp]
    for k in range(1, 8):
        rcopy(gb_own, gb_own, gb2_ss.at[0], gb2_rs.at[0], (lax.rem(dp + k, 8), s)).start()
    btot = btot[0:16]
    chs[0] = to_chans(btot, 0)
    chs[1] = to_chans(btot, 16)

    def in_step(n, _):
        for r in range(2):
            at = pl.ds(al(r * PIX + n * COLS, 32), COLS)
            cen = centred_of(x_ref[n, r].astype(F32), n)
            inner = ng[at, :] * gain - chs[0, pl.ds(n, 1), :] - cen * chs[1, pl.ds(n, 1), :]
            ig_ref[n, r] = (up_ref[n, r].astype(F32) + mcs[1, pl.ds(n, 1), :] * inner).astype(BF16)
        return 0

    lax.fori_loop(0, NIMG, in_step, 0)

    gb_most = gb2_r.at[pl.ds(0, 7)]
    rcopy(gb_most, gb_most, gb2_ss.at[0], gb2_rs.at[0], sib).wait_recv()
    totals = slot_sum(gb2_r)
    gg_ref[...] = jnp.concatenate([totals[j : j + 1] for j in range(5)], axis=1).reshape(CH)
    bg_ref[...] = jnp.concatenate([totals[5 + j : 6 + j] for j in range(5)], axis=1).reshape(CH)

    def from_me(g, i):
        p1, p2, p3 = order[g]
        return (p1 == z) & (p2 == x) & (p3 == i) & (c == ylo)

    for g in range(3):
        for i in range(4):
            @pl.when(jnp.logical_not(from_me(g, i)))
            def _():
                rcopy(y2s.at[g, 0], y2r.at[g, i], y2_ss.at[4 * g], y2_rs.at[4 * g + i], sib).wait_recv()

        total = slot_sum(y2r[g])
        for dc in range(3):
            wg_ref[3 * g + dc] = total[:, 80 * dc : 80 * (dc + 1)]

    sp_drain(*bst)
    rcopy(gb_most, gb_most, gb2_ss.at[0], gb2_rs.at[0], sib).wait_send()
    for g in range(3):
        for j in range(4):
            @pl.when(jnp.logical_not(sum3_mine(g, j)))
            def _():
                sum3(g, j).wait_send()


def finish(*refs):
    count = (len(refs) - 1) // 2
    sems = refs[-1]
    copies = [pltpu.make_async_copy(refs[i], refs[count + i], sems.at[i]) for i in range(count)]
    for copy in copies:
        copy.start()
    for copy in copies:
        copy.wait()


def body(inputs, norm_gain, norm_bias, conv_weight, upstream):
    dma = pltpu.SemaphoreType.DMA
    vm = pltpu.VMEM
    scratch = [
        vm((2, NIMG, COLS, CH), BF16),
        vm((2, NIMG, COLS, CH), BF16),
        vm((4 * PIX, 3 * CH), BF16),
        vm((4 * PIX, 3 * CH), BF16),
        vm((2, 320, OWN), BF16),
        vm((9, CH, CH), BF16),
        vm((9, 320, CH), BF16),
        vm((9, 320, CH), BF16),
        vm((9, 4, 80, CH), BF16),
        vm((9, 80, CH), F32),
        vm((4, 80, CH), F32),
        vm((3, 3, 3, 80, CH), BF16),
        vm((3, CH, 256), BF16),
        vm((3, 3, 160, 256), BF16),
        vm((CH, 256), F32),
        vm((3, 160, 256), F32),
        vm((3, 4, 40, 256), F32),
        vm((3, 4, 40, 256), F32),
        vm((OWN, CH), F32),
        vm((2, 16, CH), F32),
        vm((2, 16, CH), F32),
        vm((16, 128), F32),
        vm((16, 16, 128), F32),
        vm((32, 128), F32),
        vm((16, 32, 128), F32),
        vm((8, 16, 128), F32),
        dma((1,)), dma((1,)),
        dma((1,)), dma((1,)),
        dma((1,)), dma((1,)),
        dma((4,)), dma((4,)),
        dma((14,)), dma((14,)),
        dma((12,)), dma((12,)),
        dma((5,)), dma((5,)),
        dma((9,)), dma((9,)),
        dma((9,)), dma((9,)),
        dma((9,)), dma((9,)),
        dma((12,)), dma((12,)),
    ]
    spec = pl.BlockSpec(memory_space=pltpu.VMEM)
    results = pl.pallas_call(
        kernel,
        out_shape=(
            jax.ShapeDtypeStruct(inputs.shape, BF16),
            jax.ShapeDtypeStruct(inputs.shape, BF16),
            jax.ShapeDtypeStruct((9, 40, 80), F32),
            jax.ShapeDtypeStruct((CH,), F32),
            jax.ShapeDtypeStruct((CH,), F32),
        ),
        in_specs=[spec] * 5,
        out_specs=(spec,) * 5,
        scratch_shapes=scratch,
        compiler_params=pltpu.CompilerParams(
            collective_id=0, has_side_effects=True, vmem_limit_bytes=62 * 2**20
        ),
        name="resblock",
    )(inputs, norm_gain, norm_bias, conv_weight, upstream)
    anywhere = pl.BlockSpec(memory_space=pl.ANY)
    mixed, input_grad, wg, gain_grad, bias_grad = pl.pallas_call(
        finish,
        out_shape=tuple(jax.ShapeDtypeStruct(r.shape, r.dtype) for r in results),
        in_specs=[spec] * 5,
        out_specs=(anywhere,) * 5,
        scratch_shapes=[dma((5,))],
        name="finish",
    )(*results)
    return (mixed, input_grad, wg.transpose(0, 2, 1), gain_grad, bias_grad)


def solution(mesh):
    in_specs = (
        P("dp", "space", None, None),
        P(),
        P(),
        P(None, "dp", None),
        P("dp", "space", None, None),
    )
    out_specs = (
        P("dp", "space", None, None),
        P("dp", "space", None, None),
        P(None, "dp", "space"),
        P(),
        P(),
    )
    return jax.shard_map(body, mesh=mesh, in_specs=in_specs, out_specs=out_specs, check_vma=False)
```

```python
import functools

import jax
import jax.numpy as jnp
from jax import lax
from jax.experimental import pallas as pl
from jax.experimental.pallas import tpu as pltpu
from jax.sharding import PartitionSpec as P

GSIZE = 40
EPS = 1e-05
MESH = pl.DeviceIdType.MESH
NIMG = 14
COLS = 32
CH = 640
PIX = NIMG * COLS
OWN = 2 * PIX
COUNT = float(32 * 32 * GSIZE)
F32 = jnp.float32
BF16 = jnp.bfloat16
HIGH = lax.Precision.HIGHEST


def rcopy(src, dst, ssem, rsem, dev):
    return pltpu.make_async_remote_copy(
        src_ref=src, dst_ref=dst, send_sem=ssem, recv_sem=rsem, device_id=dev, device_id_type=MESH
    )


def al(value, unit):
    return pl.multiple_of(value, unit)


def sigmoid(v):
    return 1.0 / (1.0 + jnp.exp(-v))


def kernel(
    x_ref, gain_ref, bias_ref, w_ref, up_ref,
    mixed_ref, ig_ref, wg_ref, gg_ref, bg_ref,
    xh, uh, A3, U3, aT, W, sib_s, sib_r, s1, own1, wide, r1, x2s, x2r, wide2, own2, y2s, y2r, ng,
    chs, mcs, st_s, st_r, bst_s, bst_r, gb2_r,
    st_ss, st_rs, bst_ss, bst_rs, gb2_ss, gb2_rs,
    h_ss, h_rs, ag_ss, ag_rs, ax_ss, ax_rs, fw_ss, fw_rs,
    sib_ss, sib_rs, z_ss, z_rs, x2_ss, x2_rs, y2_ss, y2_rs,
):
    dp = lax.axis_index("dp")
    s = lax.axis_index("space")
    x = lax.div(s, 4)
    yhi = lax.rem(lax.div(s, 2), 2)
    c = lax.rem(s, 2)
    z = lax.div(dp, 2)
    ylo = lax.rem(dp, 2)
    y = yhi * 2 + ylo
    sib = (dp, s + 1 - 2 * c)

    def zdev(k):
        return (lax.rem(z + k, 4) * 2 + ylo, s)

    def xdev(k):
        return (dp, lax.rem(s + 4 * k, 16))

    def ydev(k):
        to = lax.rem(y + k, 4)
        return (z * 2 + lax.rem(to, 2), (x * 2 + lax.div(to, 2)) * 2 + c)

    bar = pltpu.get_barrier_semaphore()

    def greet(dev):
        pl.semaphore_signal(bar, inc=1, device_id=dev, device_id_type=MESH)

    for k in range(1, 16):
        greet((dp, lax.rem(s + k, 16)))
    for k in range(1, 8):
        greet((lax.rem(dp + k, 8), s))
    for a, b in ((0, 1), (1, 0), (1, 1)):
        other = (x * 2 + lax.rem(yhi + a, 2)) * 2 + lax.rem(c + b, 2)
        greet((z * 2 + 1 - ylo, other))

    def table(shape, chan_dim, shift):
        chan = lax.broadcasted_iota(jnp.int32, shape, chan_dim)
        lane = lax.broadcasted_iota(jnp.int32, shape, 1 - chan_dim) - shift
        return jnp.where((chan >= lane * GSIZE) & (chan < (lane + 1) * GSIZE), 1.0, 0.0).astype(F32)

    def to_groups(first, second):
        return jnp.dot(first, table((CH, 128), 0, 0), precision=HIGH, preferred_element_type=F32) + jnp.dot(
            second, table((CH, 128), 0, 16), precision=HIGH, preferred_element_type=F32
        )

    def to_chans(vals, shift):
        return jnp.dot(vals, table((128, CH), 1, shift), precision=HIGH, preferred_element_type=F32) / COUNT

    chs[...] = jnp.zeros_like(chs)

    def stat_step(n, _):
        v = x_ref[n].astype(F32).reshape(2 * COLS, CH)
        chs[0, pl.ds(n, 1), :] = jnp.sum(v, axis=0, keepdims=True)
        chs[1, pl.ds(n, 1), :] = jnp.sum(v * v, axis=0, keepdims=True)
        return 0

    lax.fori_loop(0, NIMG, stat_step, 0)
    stats = to_groups(chs[0], chs[1])
    st_s[...] = stats
    tb = 8 * c + (4 + x) * (1 - c)
    ta = 2 * c
    W[tb, pl.ds(al(dp * 80, 16), 80), :] = w_ref[tb]
    W[pl.ds(ta, 2), pl.ds(al(dp * 80, 16), 80), :] = w_ref[pl.ds(ta, 2)]

    def put3(dst, row, n, v, flip):
        at = pl.ds(al(row * PIX + n * COLS, 32), COLS)
        col = lax.broadcasted_iota(jnp.int32, (COLS, CH), 0)
        prev = jnp.where(col == 0, 0.0, pltpu.roll(v, 1, 0))
        after = jnp.where(col == COLS - 1, 0.0, pltpu.roll(v, COLS - 1, 0))
        first, last = (after, prev) if flip else (prev, after)
        dst[at, 0:CH] = first.astype(BF16)
        dst[at, CH : 2 * CH] = v.astype(BF16)
        dst[at, 2 * CH : 3 * CH] = last.astype(BF16)

    def up_own(n, _):
        for r in range(2):
            put3(U3, r + 1, n, up_ref[n, r].astype(F32), True)
        return 0

    lax.fori_loop(0, NIMG, up_own, 0)
    pl.semaphore_wait(bar, 25)

    def sp_start(src, dst, ssem, rsem):
        def step(k, _):
            rcopy(src, dst.at[s], ssem.at[0], rsem.at[0], (dp, lax.rem(s + k, 16))).start()
            return 0

        lax.fori_loop(1, 16, step, 0)
        dst[s] = src[...]

    def sp_wait(src, dst, ssem, rsem):
        most = dst.at[pl.ds(0, 15)]
        rcopy(most, most, ssem.at[0], rsem.at[0], sib).wait_recv()

    def sp_drain(src, dst, ssem, rsem):
        most = dst.at[pl.ds(0, 15)]
        rcopy(most, most, ssem.at[0], rsem.at[0], sib).wait_send()

    st = (st_s, st_r, st_ss, st_rs)
    sp_start(*st)

    def wsrc(j):
        return w_ref.at[pl.ds(tb, 1)] if j == 0 else w_ref.at[pl.ds(ta, 2)]

    def wrows(j, block):
        taps = pl.ds(tb, 1) if j == 0 else pl.ds(ta, 2)
        return W.at[taps, pl.ds(al(block * 80, 16), 80), :]

    ystep = ydev(1 + 2 * c)
    dpo = z * 2 + 1 - ylo

    def ag_y(j):
        return rcopy(wsrc(j), wrows(j, dp), ag_ss.at[j], ag_rs.at[j], ystep)

    def ag_z(k, j, relay):
        idx = 2 + 2 * (k - 1) + j + (6 if relay else 0)
        src = wrows(j, dpo) if relay else wsrc(j)
        return rcopy(src, wrows(j, dpo if relay else dp), ag_ss.at[idx], ag_rs.at[idx], zdev(k))

    def ag_y_recv(j):
        return rcopy(wsrc(j), wrows(j, dpo), ag_ss.at[j], ag_rs.at[j], ystep)

    def ag_z_recv(k, j, relay):
        idx = 2 + 2 * (k - 1) + j + (6 if relay else 0)
        block = lax.rem(z + 4 - k, 4) * 2 + (1 - ylo if relay else ylo)
        return rcopy(wsrc(j), wrows(j, block), ag_ss.at[idx], ag_rs.at[idx], zdev(k))

    def ax(k, m):
        rows = pl.ds(al(lax.rem(z + 4 - m, 4) * 160, 16), 160)
        i = 4 * (k - 1) + m
        return rcopy(W.at[4 + x, rows], W.at[4 + x, rows], ax_ss.at[i], ax_rs.at[i], xdev(k))

    def ax_recv(k, m):
        rows = pl.ds(al(lax.rem(z + 4 - m, 4) * 160, 16), 160)
        i = 4 * (k - 1) + m
        tap = 4 + lax.rem(x + 4 - k, 4)
        return rcopy(W.at[tap, rows], W.at[tap, rows], ax_ss.at[i], ax_rs.at[i], xdev(k))

    def ax_send(m):
        @pl.when(c == 0)
        def _():
            for k in (1, 3, 2):
                ax(k, m).start()

    def fw_a(far):
        taps = pl.ds(2 - ta if far else ta, 2)
        return rcopy(W.at[taps], W.at[taps], fw_ss.at[0], fw_rs.at[0], sib)

    def fw_b(tap, i):
        return rcopy(W.at[tap], W.at[tap], fw_ss.at[i], fw_rs.at[i], sib)

    for j in range(2):
        ag_y(j).start()

    above = (dp, lax.rem(s + 15, 16))
    below = (dp, lax.rem(s + 1, 16))

    def halo(i):
        ref, dst = (up_ref, uh) if i < 2 else (x_ref, xh)
        if i % 2 == 0:
            return rcopy(ref.at[:, 0], dst.at[1], h_ss.at[i], h_rs.at[i], above)
        return rcopy(ref.at[:, 1], dst.at[0], h_ss.at[i], h_rs.at[i], below)

    for i in range(2):
        halo(i).start()
    for j in range(2):
        for k in (1, 3, 2):
            ag_z(k, j, False).start()


    for j in range(2):
        ag_y_recv(j).wait_recv()
        for k in (1, 3, 2):
            ag_z(k, j, True).start()
        if j == 0:
            ax_send(0)

    sp_wait(*st)

    def slot_sum(ref):
        total = ref[0]
        for i in range(1, ref.shape[0]):
            total = total + ref[i]
        return total

    tot = slot_sum(st_r)
    mean = to_chans(tot, 0)
    mcs[0] = mean
    mcs[1] = lax.rsqrt(to_chans(tot, 16) - mean * mean + EPS)
    gain = gain_ref[...].reshape(1, CH)
    bias = bias_ref[...].reshape(1, CH)

    def centred_of(v, n):
        return (v - mcs[0, pl.ds(n, 1), :]) * mcs[1, pl.ds(n, 1), :]

    def act_of(v, n):
        normed = centred_of(v, n) * gain + bias
        return normed * sigmoid(normed)

    def act_own(n, _):
        for r in range(2):
            put3(A3, r + 1, n, act_of(x_ref[n, r].astype(F32), n), False)
        return 0

    lax.fori_loop(0, NIMG, act_own, 0)

    def turn(m, _):
        block = A3[pl.ds(al(PIX + m * 128, 16), 128), CH : 2 * CH].astype(F32).T.astype(BF16)
        for q in range(4):
            for p in range(2):
                d = 2 * q + p
                aT[p, q * 80 : (q + 1) * 80, pl.ds(al(m * 128, 128), 128)] = block[d * 80 : (d + 1) * 80]
        return 0

    lax.fori_loop(0, OWN // 128, turn, 0)

    def terms(p, dr, dc):
        rhs = U3[pl.ds(al((2 - dr) * PIX, 16), OWN), dc * CH : (dc + 1) * CH]
        return jnp.dot(aT[p], rhs, preferred_element_type=F32)

    def sib_copy(t):
        return rcopy(sib_s.at[t], sib_r.at[t], sib_ss.at[t], sib_rs.at[t], sib)

    def far_terms(dr):
        for dc in range(3):
            t = 3 * dr + dc
            sib_s[t] = terms(1 - c, dr, dc).astype(BF16)
            sib_copy(t).start()

    axes = ((zdev, xdev), (xdev, ydev), (ydev, zdev))
    order = ((z, x, y), (x, y, z), (y, z, x))

    def sum1(g, k):
        i = 3 * g + k - 1
        to = lax.rem(order[g][0] + k, 4)
        return rcopy(s1.at[pl.ds(3 * g, 3), to], r1.at[g, k - 1], z_ss.at[i], z_rs.at[i], axes[g][0](k))

    def near_terms(dr):
        for dc in range(3):
            t = 3 * dr + dc
            near = terms(c, dr, dc)
            sib_copy(t).wait_recv()
            near = (near + sib_r[t].astype(F32)).reshape(4, 80, CH)
            s1[t] = near.astype(BF16)
            wide[...] = near
            own1[t] = wide[order[dr][0]]
        for k in (1, 3, 2):
            sum1(dr, k).start()

    for k in (1, 3, 2):
        ag_z_recv(k, 0, False).wait_recv()
        ag_z_recv(k, 0, True).wait_recv()
        ax_send(k)
    fw_b(tb, 1).start()

    far_terms(1)
    near_terms(1)

    for i in range(2):
        halo(i).wait_recv()

    def masked(v, edge):
        return jnp.where(s == (0 if edge == 0 else 15), jnp.zeros_like(v), v)

    def up_halo(n, _):
        for e in range(2):
            put3(U3, 3 * e, n, masked(uh[e, n].astype(F32), e), True)
        return 0

    for i in range(2, 4):
        halo(i).start()
    lax.fori_loop(0, NIMG, up_halo, 0)

    far_terms(0)
    far_terms(2)
    near_terms(0)
    near_terms(2)

    for k in (1, 3, 2):
        ag_z_recv(k, 1, False).wait_recv()
        ag_z_recv(k, 1, True).wait_recv()
    fw_a(False).start()

    @pl.when(c == 0)
    def _():
        for k in (1, 3, 2):
            for m in range(4):
                ax_recv(k, m).wait_recv()
            fw_b(4 + lax.rem(x + 4 - k, 4), 1 + k).start()
        fw_b(8, 1).wait_recv()

    @pl.when(c == 1)
    def _():
        fw_b(4 + x, 1).wait_recv()
        for k in (1, 3, 2):
            fw_b(4 + lax.rem(x + 4 - k, 4), 1 + k).wait_recv()

    fw_a(True).wait_recv()

    def sum2(g, k):
        i = 3 * g + k - 1
        rows = pl.ds(al(lax.rem(order[g][1] + k, 4) * 160, 16), 160)
        return rcopy(x2s.at[g, rows, :], x2r.at[g, k - 1], x2_ss.at[i], x2_rs.at[i], axes[g][1](k))

    def stage2(g):
        total = own1[3 * g : 3 * g + 3]
        for k in (1, 3, 2):
            sum1(g, k).wait_recv()
            total = total + r1[g, k - 1].astype(F32)
        total = jnp.concatenate([total.reshape(240, CH), jnp.zeros((16, CH), F32)], axis=0).T
        wide2[...] = total
        own2[g] = wide2[pl.ds(al(order[g][1] * 160, 16), 160), :]
        x2s[g] = total.astype(BF16)
        for k in (1, 3, 2):
            sum2(g, k).start()

    def sum3(g, j):
        i = 4 * g + j
        return rcopy(
            y2s.at[g, j], y2r.at[g, order[g][2]], y2_ss.at[i], y2_rs.at[4 * g + order[g][2]],
            (order[g][0] * 2 + c, order[g][1] * 4 + j),
        )

    def sum3_mine(g, j):
        return (order[g][0] * 2 + c == dp) & (order[g][1] * 4 + j == s)

    def stage3(g):
        total = own2[g]
        for k in (1, 3, 2):
            sum2(g, k).wait_recv()
            total = total + x2r[g, k - 1].astype(F32)
        for j in range(4):
            y2s[g, j] = total[40 * j : 40 * (j + 1), :]
        for j in range(4):
            @pl.when(jnp.logical_not(sum3_mine(g, j)))
            def _():
                sum3(g, j).start()

            @pl.when(sum3_mine(g, j))
            def _():
                y2r[g, order[g][2]] = y2s[g, j]

    def grad_step(r, _):
        total = None
        for dr in range(3):
            for dc in range(3):
                t = 3 * dr + dc
                part = lax.dot_general(
                    U3[pl.ds(al((r + 2 - dr) * PIX, 16), PIX), dc * CH : (dc + 1) * CH],
                    W[t],
                    (((1,), (1,)), ((), ())),
                    preferred_element_type=F32,
                )
                total = part if total is None else total + part
        ng[pl.ds(al(r * PIX, 16), PIX), :] = total
        return 0

    grad_step(0, 0)
    stage2(1)
    grad_step(1, 0)

    def norm_step(n, _):
        first = jnp.zeros((1, CH), F32)
        second = jnp.zeros((1, CH), F32)
        for r in range(2):
            at = pl.ds(al(r * PIX + n * COLS, 32), COLS)
            cen = centred_of(x_ref[n, r].astype(F32), n)
            normed = cen * gain + bias
            sg = sigmoid(normed)
            grad = ng[at, :] * sg * (1.0 + normed * (1.0 - sg))
            ng[at, :] = grad
            first = first + jnp.sum(grad, axis=0, keepdims=True)
            second = second + jnp.sum(grad * cen, axis=0, keepdims=True)
        chs[0, pl.ds(n, 1), :] = first
        chs[1, pl.ds(n, 1), :] = second
        return 0

    lax.fori_loop(0, NIMG, norm_step, 0)
    bst_s[0:16] = to_groups(chs[0] * gain, chs[1] * gain)
    for i in range(2):
        part = jnp.sum(chs[1 - i], axis=0, keepdims=True)
        for j in range(5):
            bst_s[16 + 5 * i + j : 17 + 5 * i + j] = part[:, 128 * j : 128 * (j + 1)]
    bst_s[26:32] = jnp.zeros((6, 128), F32)
    bst = (bst_s, bst_r, bst_ss, bst_rs)
    sp_start(*bst)

    stage2(0)
    stage2(2)

    for i in range(2, 4):
        halo(i).wait_recv()

    def act_halo(n, _):
        for e in range(2):
            put3(A3, 3 * e, n, masked(act_of(xh[e, n].astype(F32), n), e), False)
        return 0

    lax.fori_loop(0, NIMG, act_halo, 0)

    def conv_step(r, _):
        total = None
        for dr in range(3):
            part = jnp.dot(
                A3[pl.ds(al((r + dr) * PIX, 16), PIX), :],
                W[3 * dr : 3 * dr + 3].reshape(3 * CH, CH),
                preferred_element_type=F32,
            )
            total = part if total is None else total + part
        mixed_ref[:, r] = (x_ref[:, r].astype(F32) + total.reshape(NIMG, COLS, CH)).astype(BF16)
        return 0

    stage3(1)
    conv_step(0, 0)
    stage3(0)
    stage3(2)

    conv_step(1, 0)

    sp_drain(*st)
    for j in range(2):
        ag_y(j).wait_send()
        for k in range(1, 4):
            ag_z(k, j, False).wait_send()
            ag_z(k, j, True).wait_send()
    for i in range(4):
        halo(i).wait_send()
    fw_a(False).wait_send()
    fw_b(tb, 1).wait_send()

    @pl.when(c == 0)
    def _():
        for k in range(1, 4):
            for m in range(4):
                ax(k, m).wait_send()
            fw_b(4 + x, 1 + k).wait_send()


    def sib_drain(t, _):
        sib_copy(t).wait_send()
        return 0

    lax.fori_loop(0, 9, sib_drain, 0)

    for g in range(3):
        for k in range(1, 4):
            sum1(g, k).wait_send()
            sum2(g, k).wait_send()

    sp_wait(*bst)
    btot = slot_sum(bst_r)
    gb2_r[dp] = btot[16:32]
    gb_own = gb2_r.at[dp]
    for k in range(1, 8):
        rcopy(gb_own, gb_own, gb2_ss.at[0], gb2_rs.at[0], (lax.rem(dp + k, 8), s)).start()
    btot = btot[0:16]
    chs[0] = to_chans(btot, 0)
    chs[1] = to_chans(btot, 16)

    def in_step(n, _):
        for r in range(2):
            at = pl.ds(al(r * PIX + n * COLS, 32), COLS)
            cen = centred_of(x_ref[n, r].astype(F32), n)
            inner = ng[at, :] * gain - chs[0, pl.ds(n, 1), :] - cen * chs[1, pl.ds(n, 1), :]
            ig_ref[n, r] = (up_ref[n, r].astype(F32) + mcs[1, pl.ds(n, 1), :] * inner).astype(BF16)
        return 0

    lax.fori_loop(0, NIMG, in_step, 0)

    gb_most = gb2_r.at[pl.ds(0, 7)]
    rcopy(gb_most, gb_most, gb2_ss.at[0], gb2_rs.at[0], sib).wait_recv()
    totals = slot_sum(gb2_r)
    gg_ref[...] = jnp.concatenate([totals[j : j + 1] for j in range(5)], axis=1).reshape(CH)
    bg_ref[...] = jnp.concatenate([totals[5 + j : 6 + j] for j in range(5)], axis=1).reshape(CH)

    def from_me(g, i):
        p1, p2, p3 = order[g]
        return (p1 == z) & (p2 == x) & (p3 == i) & (c == ylo)

    for g in range(3):
        for i in range(4):
            @pl.when(jnp.logical_not(from_me(g, i)))
            def _():
                rcopy(y2s.at[g, 0], y2r.at[g, i], y2_ss.at[4 * g], y2_rs.at[4 * g + i], sib).wait_recv()

        total = slot_sum(y2r[g])
        for dc in range(3):
            wg_ref[3 * g + dc] = total[:, 80 * dc : 80 * (dc + 1)]

    sp_drain(*bst)
    rcopy(gb_most, gb_most, gb2_ss.at[0], gb2_rs.at[0], sib).wait_send()
    for g in range(3):
        for j in range(4):
            @pl.when(jnp.logical_not(sum3_mine(g, j)))
            def _():
                sum3(g, j).wait_send()


def finish(*refs):
    count = (len(refs) - 1) // 2
    sems = refs[-1]
    copies = [pltpu.make_async_copy(refs[i], refs[count + i], sems.at[i]) for i in range(count)]
    for copy in copies:
        copy.start()
    for copy in copies:
        copy.wait()


def body(inputs, norm_gain, norm_bias, conv_weight, upstream):
    dma = pltpu.SemaphoreType.DMA
    vm = pltpu.VMEM
    scratch = [
        vm((2, NIMG, COLS, CH), BF16),
        vm((2, NIMG, COLS, CH), BF16),
        vm((4 * PIX, 3 * CH), BF16),
        vm((4 * PIX, 3 * CH), BF16),
        vm((2, 320, OWN), BF16),
        vm((9, CH, CH), BF16),
        vm((9, 320, CH), BF16),
        vm((9, 320, CH), BF16),
        vm((9, 4, 80, CH), BF16),
        vm((9, 80, CH), F32),
        vm((4, 80, CH), F32),
        vm((3, 3, 3, 80, CH), BF16),
        vm((3, CH, 256), BF16),
        vm((3, 3, 160, 256), BF16),
        vm((CH, 256), F32),
        vm((3, 160, 256), F32),
        vm((3, 4, 40, 256), F32),
        vm((3, 4, 40, 256), F32),
        vm((OWN, CH), F32),
        vm((2, 16, CH), F32),
        vm((2, 16, CH), F32),
        vm((16, 128), F32),
        vm((16, 16, 128), F32),
        vm((32, 128), F32),
        vm((16, 32, 128), F32),
        vm((8, 16, 128), F32),
        dma((1,)), dma((1,)),
        dma((1,)), dma((1,)),
        dma((1,)), dma((1,)),
        dma((4,)), dma((4,)),
        dma((14,)), dma((14,)),
        dma((12,)), dma((12,)),
        dma((5,)), dma((5,)),
        dma((9,)), dma((9,)),
        dma((9,)), dma((9,)),
        dma((9,)), dma((9,)),
        dma((12,)), dma((12,)),
    ]
    spec = pl.BlockSpec(memory_space=pltpu.VMEM)
    results = pl.pallas_call(
        kernel,
        out_shape=(
            jax.ShapeDtypeStruct(inputs.shape, BF16),
            jax.ShapeDtypeStruct(inputs.shape, BF16),
            jax.ShapeDtypeStruct((9, 40, 80), F32),
            jax.ShapeDtypeStruct((CH,), F32),
            jax.ShapeDtypeStruct((CH,), F32),
        ),
        in_specs=[spec] * 5,
        out_specs=(spec,) * 5,
        scratch_shapes=scratch,
        compiler_params=pltpu.CompilerParams(
            collective_id=0, has_side_effects=True, vmem_limit_bytes=62 * 2**20
        ),
        name="resblock",
    )(inputs, norm_gain, norm_bias, conv_weight, upstream)
    anywhere = pl.BlockSpec(memory_space=pl.ANY)
    mixed, input_grad, wg, gain_grad, bias_grad = pl.pallas_call(
        finish,
        out_shape=tuple(jax.ShapeDtypeStruct(r.shape, r.dtype) for r in results),
        in_specs=[spec] * 5,
        out_specs=(anywhere,) * 5,
        scratch_shapes=[dma((5,))],
        name="finish",
    )(*results)
    return (mixed, input_grad, wg.transpose(0, 2, 1), gain_grad, bias_grad)


def solution(mesh):
    in_specs = (
        P("dp", "space", None, None),
        P(),
        P(),
        P(None, "dp", None),
        P("dp", "space", None, None),
    )
    out_specs = (
        P("dp", "space", None, None),
        P("dp", "space", None, None),
        P(None, "dp", "space"),
        P(),
        P(),
    )
    return jax.shard_map(body, mesh=mesh, in_specs=in_specs, out_specs=out_specs, check_vma=False)
```

```python
import functools

import jax
import jax.numpy as jnp
from jax import lax
from jax.experimental import pallas as pl
from jax.experimental.pallas import tpu as pltpu
from jax.sharding import PartitionSpec as P

GSIZE = 40
EPS = 1e-05
MESH = pl.DeviceIdType.MESH
NIMG = 14
COLS = 32
CH = 640
PIX = NIMG * COLS
OWN = 2 * PIX
COUNT = float(32 * 32 * GSIZE)
F32 = jnp.float32
BF16 = jnp.bfloat16
HIGH = lax.Precision.HIGHEST


def rcopy(src, dst, ssem, rsem, dev):
    return pltpu.make_async_remote_copy(
        src_ref=src, dst_ref=dst, send_sem=ssem, recv_sem=rsem, device_id=dev, device_id_type=MESH
    )


def al(value, unit):
    return pl.multiple_of(value, unit)


def sigmoid(v):
    return 1.0 / (1.0 + jnp.exp(-v))


def kernel(
    x_ref, gain_ref, bias_ref, w_ref, up_ref,
    mixed_ref, ig_ref, wg_ref, gg_ref, bg_ref,
    xh, uh, A3, U3, aT, W, sib_s, sib_r, s1, own1, wide, r1, x2s, x2r, wide2, own2, y2s, y2r, ng,
    chs, mcs, st_s, st_r, bst_s, bst_r, gb2_r,
    st_ss, st_rs, bst_ss, bst_rs, gb2_ss, gb2_rs,
    h_ss, h_rs, ag_ss, ag_rs, ax_ss, ax_rs, fw_ss, fw_rs,
    sib_ss, sib_rs, z_ss, z_rs, x2_ss, x2_rs, y2_ss, y2_rs,
):
    dp = lax.axis_index("dp")
    s = lax.axis_index("space")
    x = lax.div(s, 4)
    yhi = lax.rem(lax.div(s, 2), 2)
    c = lax.rem(s, 2)
    z = lax.div(dp, 2)
    ylo = lax.rem(dp, 2)
    y = yhi * 2 + ylo
    sib = (dp, s + 1 - 2 * c)

    def zdev(k):
        return (lax.rem(z + k, 4) * 2 + ylo, s)

    def xdev(k):
        return (dp, lax.rem(s + 4 * k, 16))

    def ydev(k):
        to = lax.rem(y + k, 4)
        return (z * 2 + lax.rem(to, 2), (x * 2 + lax.div(to, 2)) * 2 + c)

    bar = pltpu.get_barrier_semaphore()

    def greet(dev):
        pl.semaphore_signal(bar, inc=1, device_id=dev, device_id_type=MESH)

    for k in range(1, 16):
        greet((dp, lax.rem(s + k, 16)))
    for k in range(1, 8):
        greet((lax.rem(dp + k, 8), s))
    for a, b in ((0, 1), (1, 0), (1, 1)):
        other = (x * 2 + lax.rem(yhi + a, 2)) * 2 + lax.rem(c + b, 2)
        greet((z * 2 + 1 - ylo, other))

    def table(shape, chan_dim, shift):
        chan = lax.broadcasted_iota(jnp.int32, shape, chan_dim)
        lane = lax.broadcasted_iota(jnp.int32, shape, 1 - chan_dim) - shift
        return jnp.where((chan >= lane * GSIZE) & (chan < (lane + 1) * GSIZE), 1.0, 0.0).astype(F32)

    def to_groups(first, second):
        return jnp.dot(first, table((CH, 128), 0, 0), precision=HIGH, preferred_element_type=F32) + jnp.dot(
            second, table((CH, 128), 0, 16), precision=HIGH, preferred_element_type=F32
        )

    def to_chans(vals, shift):
        return jnp.dot(vals, table((128, CH), 1, shift), precision=HIGH, preferred_element_type=F32) / COUNT

    chs[...] = jnp.zeros_like(chs)

    def stat_step(n, _):
        v = x_ref[n].astype(F32).reshape(2 * COLS, CH)
        chs[0, pl.ds(n, 1), :] = jnp.sum(v, axis=0, keepdims=True)
        chs[1, pl.ds(n, 1), :] = jnp.sum(v * v, axis=0, keepdims=True)
        return 0

    lax.fori_loop(0, NIMG, stat_step, 0)
    stats = to_groups(chs[0], chs[1])
    st_s[...] = stats
    tb = 8 * c + (4 + x) * (1 - c)
    ta = 2 * c
    W[tb, pl.ds(al(dp * 80, 16), 80), :] = w_ref[tb]
    W[pl.ds(ta, 2), pl.ds(al(dp * 80, 16), 80), :] = w_ref[pl.ds(ta, 2)]

    def put3(dst, row, n, v, flip):
        at = pl.ds(al(row * PIX + n * COLS, 32), COLS)
        col = lax.broadcasted_iota(jnp.int32, (COLS, CH), 0)
        prev = jnp.where(col == 0, 0.0, pltpu.roll(v, 1, 0))
        after = jnp.where(col == COLS - 1, 0.0, pltpu.roll(v, COLS - 1, 0))
        first, last = (after, prev) if flip else (prev, after)
        dst[at, 0:CH] = first.astype(BF16)
        dst[at, CH : 2 * CH] = v.astype(BF16)
        dst[at, 2 * CH : 3 * CH] = last.astype(BF16)

    def up_own(n, _):
        for r in range(2):
            put3(U3, r + 1, n, up_ref[n, r].astype(F32), True)
        return 0

    lax.fori_loop(0, NIMG, up_own, 0)
    pl.semaphore_wait(bar, 25)

    def sp_start(src, dst, ssem, rsem):
        def step(k, _):
            rcopy(src, dst.at[s], ssem.at[0], rsem.at[0], (dp, lax.rem(s + k, 16))).start()
            return 0

        lax.fori_loop(1, 16, step, 0)
        dst[s] = src[...]

    def sp_wait(src, dst, ssem, rsem):
        most = dst.at[pl.ds(0, 15)]
        rcopy(most, most, ssem.at[0], rsem.at[0], sib).wait_recv()

    def sp_drain(src, dst, ssem, rsem):
        most = dst.at[pl.ds(0, 15)]
        rcopy(most, most, ssem.at[0], rsem.at[0], sib).wait_send()

    st = (st_s, st_r, st_ss, st_rs)
    sp_start(*st)

    def wsrc(j):
        return w_ref.at[pl.ds(tb, 1)] if j == 0 else w_ref.at[pl.ds(ta, 2)]

    def wrows(j, block):
        taps = pl.ds(tb, 1) if j == 0 else pl.ds(ta, 2)
        return W.at[taps, pl.ds(al(block * 80, 16), 80), :]

    ystep = ydev(1 + 2 * c)
    dpo = z * 2 + 1 - ylo

    def ag_y(j):
        return rcopy(wsrc(j), wrows(j, dp), ag_ss.at[j], ag_rs.at[j], ystep)

    def ag_z(k, j, relay):
        idx = 2 + 2 * (k - 1) + j + (6 if relay else 0)
        src = wrows(j, dpo) if relay else wsrc(j)
        return rcopy(src, wrows(j, dpo if relay else dp), ag_ss.at[idx], ag_rs.at[idx], zdev(k))

    def ag_y_recv(j):
        return rcopy(wsrc(j), wrows(j, dpo), ag_ss.at[j], ag_rs.at[j], ystep)

    def ag_z_recv(k, j, relay):
        idx = 2 + 2 * (k - 1) + j + (6 if relay else 0)
        block = lax.rem(z + 4 - k, 4) * 2 + (1 - ylo if relay else ylo)
        return rcopy(wsrc(j), wrows(j, block), ag_ss.at[idx], ag_rs.at[idx], zdev(k))

    def ax(k, m):
        rows = pl.ds(al(lax.rem(z + 4 - m, 4) * 160, 16), 160)
        i = 4 * (k - 1) + m
        return rcopy(W.at[4 + x, rows], W.at[4 + x, rows], ax_ss.at[i], ax_rs.at[i], xdev(k))

    def ax_recv(k, m):
        rows = pl.ds(al(lax.rem(z + 4 - m, 4) * 160, 16), 160)
        i = 4 * (k - 1) + m
        tap = 4 + lax.rem(x + 4 - k, 4)
        return rcopy(W.at[tap, rows], W.at[tap, rows], ax_ss.at[i], ax_rs.at[i], xdev(k))

    def ax_send(m):
        @pl.when(c == 0)
        def _():
            for k in (1, 3, 2):
                ax(k, m).start()

    def fw_a(far):
        taps = pl.ds(2 - ta if far else ta, 2)
        return rcopy(W.at[taps], W.at[taps], fw_ss.at[0], fw_rs.at[0], sib)

    def fw_b(tap, i):
        return rcopy(W.at[tap], W.at[tap], fw_ss.at[i], fw_rs.at[i], sib)

    for j in range(2):
        ag_y(j).start()

    above = (dp, lax.rem(s + 15, 16))
    below = (dp, lax.rem(s + 1, 16))

    def halo(i):
        ref, dst = (up_ref, uh) if i < 2 else (x_ref, xh)
        if i % 2 == 0:
            return rcopy(ref.at[:, 0], dst.at[1], h_ss.at[i], h_rs.at[i], above)
        return rcopy(ref.at[:, 1], dst.at[0], h_ss.at[i], h_rs.at[i], below)

    for i in range(2):
        halo(i).start()
    for j in range(2):
        for k in (1, 3, 2):
            ag_z(k, j, False).start()


    for j in range(2):
        ag_y_recv(j).wait_recv()
        for k in (1, 3, 2):
            ag_z(k, j, True).start()
        if j == 0:
            ax_send(0)

    sp_wait(*st)

    def slot_sum(ref):
        total = ref[0]
        for i in range(1, ref.shape[0]):
            total = total + ref[i]
        return total

    tot = slot_sum(st_r)
    mean = to_chans(tot, 0)
    mcs[0] = mean
    mcs[1] = lax.rsqrt(to_chans(tot, 16) - mean * mean + EPS)
    gain = gain_ref[...].reshape(1, CH)
    bias = bias_ref[...].reshape(1, CH)

    def centred_of(v, n):
        return (v - mcs[0, pl.ds(n, 1), :]) * mcs[1, pl.ds(n, 1), :]

    def act_of(v, n):
        normed = centred_of(v, n) * gain + bias
        return normed * sigmoid(normed)

    def act_own(n, _):
        for r in range(2):
            put3(A3, r + 1, n, act_of(x_ref[n, r].astype(F32), n), False)
        return 0

    lax.fori_loop(0, NIMG, act_own, 0)

    def turn(m, _):
        block = A3[pl.ds(al(PIX + m * 128, 16), 128), CH : 2 * CH].astype(F32).T.astype(BF16)
        for q in range(4):
            for p in range(2):
                d = 2 * q + p
                aT[p, q * 80 : (q + 1) * 80, pl.ds(al(m * 128, 128), 128)] = block[d * 80 : (d + 1) * 80]
        return 0

    lax.fori_loop(0, OWN // 128, turn, 0)

    def terms(p, dr, dc):
        rhs = U3[pl.ds(al((2 - dr) * PIX, 16), OWN), dc * CH : (dc + 1) * CH]
        return jnp.dot(aT[p], rhs, preferred_element_type=F32)

    def sib_copy(t):
        return rcopy(sib_s.at[t], sib_r.at[t], sib_ss.at[t], sib_rs.at[t], sib)

    def far_terms(dr):
        for dc in range(3):
            t = 3 * dr + dc
            sib_s[t] = terms(1 - c, dr, dc).astype(BF16)
            sib_copy(t).start()

    axes = ((zdev, xdev), (xdev, ydev), (ydev, zdev))
    order = ((z, x, y), (x, y, z), (y, z, x))

    def sum1(g, k):
        i = 3 * g + k - 1
        to = lax.rem(order[g][0] + k, 4)
        return rcopy(s1.at[pl.ds(3 * g, 3), to], r1.at[g, k - 1], z_ss.at[i], z_rs.at[i], axes[g][0](k))

    def near_terms(dr):
        for dc in range(3):
            t = 3 * dr + dc
            near = terms(c, dr, dc)
            sib_copy(t).wait_recv()
            near = (near + sib_r[t].astype(F32)).reshape(4, 80, CH)
            s1[t] = near.astype(BF16)
            wide[...] = near
            own1[t] = wide[order[dr][0]]
        for k in (1, 3, 2):
            sum1(dr, k).start()

    for k in (1, 3, 2):
        ag_z_recv(k, 0, False).wait_recv()
        ag_z_recv(k, 0, True).wait_recv()
        ax_send(k)
    fw_b(tb, 1).start()

    far_terms(1)
    near_terms(1)

    for i in range(2):
        halo(i).wait_recv()

    def masked(v, edge):
        return jnp.where(s == (0 if edge == 0 else 15), jnp.zeros_like(v), v)

    def up_halo(n, _):
        for e in range(2):
            put3(U3, 3 * e, n, masked(uh[e, n].astype(F32), e), True)
        return 0

    for i in range(2, 4):
        halo(i).start()
    lax.fori_loop(0, NIMG, up_halo, 0)

    far_terms(0)
    near_terms(0)
    far_terms(2)
    near_terms(2)

    for k in (1, 3, 2):
        ag_z_recv(k, 1, False).wait_recv()
        ag_z_recv(k, 1, True).wait_recv()
    fw_a(False).start()

    @pl.when(c == 0)
    def _():
        for k in (1, 3, 2):
            for m in range(4):
                ax_recv(k, m).wait_recv()
            fw_b(4 + lax.rem(x + 4 - k, 4), 1 + k).start()
        fw_b(8, 1).wait_recv()

    @pl.when(c == 1)
    def _():
        fw_b(4 + x, 1).wait_recv()
        for k in (1, 3, 2):
            fw_b(4 + lax.rem(x + 4 - k, 4), 1 + k).wait_recv()

    fw_a(True).wait_recv()

    def sum2(g, k):
        i = 3 * g + k - 1
        rows = pl.ds(al(lax.rem(order[g][1] + k, 4) * 160, 16), 160)
        return rcopy(x2s.at[g, rows, :], x2r.at[g, k - 1], x2_ss.at[i], x2_rs.at[i], axes[g][1](k))

    def stage2(g):
        total = own1[3 * g : 3 * g + 3]
        for k in (1, 3, 2):
            sum1(g, k).wait_recv()
            total = total + r1[g, k - 1].astype(F32)
        total = jnp.concatenate([total.reshape(240, CH), jnp.zeros((16, CH), F32)], axis=0).T
        wide2[...] = total
        own2[g] = wide2[pl.ds(al(order[g][1] * 160, 16), 160), :]
        x2s[g] = total.astype(BF16)
        for k in (1, 3, 2):
            sum2(g, k).start()

    def sum3(g, j):
        i = 4 * g + j
        return rcopy(
            y2s.at[g, j], y2r.at[g, order[g][2]], y2_ss.at[i], y2_rs.at[4 * g + order[g][2]],
            (order[g][0] * 2 + c, order[g][1] * 4 + j),
        )

    def sum3_mine(g, j):
        return (order[g][0] * 2 + c == dp) & (order[g][1] * 4 + j == s)

    def stage3(g):
        total = own2[g]
        for k in (1, 3, 2):
            sum2(g, k).wait_recv()
            total = total + x2r[g, k - 1].astype(F32)
        for j in range(4):
            y2s[g, j] = total[40 * j : 40 * (j + 1), :]
        for j in range(4):
            @pl.when(jnp.logical_not(sum3_mine(g, j)))
            def _():
                sum3(g, j).start()

            @pl.when(sum3_mine(g, j))
            def _():
                y2r[g, order[g][2]] = y2s[g, j]

    def grad_step(r, _):
        total = None
        for dr in range(3):
            for dc in range(3):
                t = 3 * dr + dc
                part = lax.dot_general(
                    U3[pl.ds(al((r + 2 - dr) * PIX, 16), PIX), dc * CH : (dc + 1) * CH],
                    W[t],
                    (((1,), (1,)), ((), ())),
                    preferred_element_type=F32,
                )
                total = part if total is None else total + part
        ng[pl.ds(al(r * PIX, 16), PIX), :] = total
        return 0

    grad_step(0, 0)
    stage2(1)
    grad_step(1, 0)

    def norm_step(n, _):
        first = jnp.zeros((1, CH), F32)
        second = jnp.zeros((1, CH), F32)
        for r in range(2):
            at = pl.ds(al(r * PIX + n * COLS, 32), COLS)
            cen = centred_of(x_ref[n, r].astype(F32), n)
            normed = cen * gain + bias
            sg = sigmoid(normed)
            grad = ng[at, :] * sg * (1.0 + normed * (1.0 - sg))
            ng[at, :] = grad
            first = first + jnp.sum(grad, axis=0, keepdims=True)
            second = second + jnp.sum(grad * cen, axis=0, keepdims=True)
        chs[0, pl.ds(n, 1), :] = first
        chs[1, pl.ds(n, 1), :] = second
        return 0

    lax.fori_loop(0, NIMG, norm_step, 0)
    bst_s[0:16] = to_groups(chs[0] * gain, chs[1] * gain)
    for i in range(2):
        part = jnp.sum(chs[1 - i], axis=0, keepdims=True)
        for j in range(5):
            bst_s[16 + 5 * i + j : 17 + 5 * i + j] = part[:, 128 * j : 128 * (j + 1)]
    bst_s[26:32] = jnp.zeros((6, 128), F32)
    bst = (bst_s, bst_r, bst_ss, bst_rs)
    sp_start(*bst)

    stage2(0)
    stage2(2)

    for i in range(2, 4):
        halo(i).wait_recv()

    def act_halo(n, _):
        for e in range(2):
            put3(A3, 3 * e, n, masked(act_of(xh[e, n].astype(F32), n), e), False)
        return 0

    lax.fori_loop(0, NIMG, act_halo, 0)

    def conv_step(r, _):
        total = None
        for dr in range(3):
            part = jnp.dot(
                A3[pl.ds(al((r + dr) * PIX, 16), PIX), :],
                W[3 * dr : 3 * dr + 3].reshape(3 * CH, CH),
                preferred_element_type=F32,
            )
            total = part if total is None else total + part
        mixed_ref[:, r] = (x_ref[:, r].astype(F32) + total.reshape(NIMG, COLS, CH)).astype(BF16)
        return 0

    stage3(1)
    conv_step(0, 0)
    stage3(0)
    stage3(2)

    conv_step(1, 0)

    sp_drain(*st)
    for j in range(2):
        ag_y(j).wait_send()
        for k in range(1, 4):
            ag_z(k, j, False).wait_send()
            ag_z(k, j, True).wait_send()
    for i in range(4):
        halo(i).wait_send()
    fw_a(False).wait_send()
    fw_b(tb, 1).wait_send()

    @pl.when(c == 0)
    def _():
        for k in range(1, 4):
            for m in range(4):
                ax(k, m).wait_send()
            fw_b(4 + x, 1 + k).wait_send()


    def sib_drain(t, _):
        sib_copy(t).wait_send()
        return 0

    lax.fori_loop(0, 9, sib_drain, 0)

    for g in range(3):
        for k in range(1, 4):
            sum1(g, k).wait_send()
            sum2(g, k).wait_send()

    sp_wait(*bst)
    btot = slot_sum(bst_r)
    gb2_r[dp] = btot[16:32]
    gb_own = gb2_r.at[dp]
    for k in range(1, 8):
        rcopy(gb_own, gb_own, gb2_ss.at[0], gb2_rs.at[0], (lax.rem(dp + k, 8), s)).start()
    btot = btot[0:16]
    chs[0] = to_chans(btot, 0)
    chs[1] = to_chans(btot, 16)

    def in_step(n, _):
        for r in range(2):
            at = pl.ds(al(r * PIX + n * COLS, 32), COLS)
            cen = centred_of(x_ref[n, r].astype(F32), n)
            inner = ng[at, :] * gain - chs[0, pl.ds(n, 1), :] - cen * chs[1, pl.ds(n, 1), :]
            ig_ref[n, r] = (up_ref[n, r].astype(F32) + mcs[1, pl.ds(n, 1), :] * inner).astype(BF16)
        return 0

    lax.fori_loop(0, NIMG, in_step, 0)

    gb_most = gb2_r.at[pl.ds(0, 7)]
    rcopy(gb_most, gb_most, gb2_ss.at[0], gb2_rs.at[0], sib).wait_recv()
    totals = slot_sum(gb2_r)
    gg_ref[...] = jnp.concatenate([totals[j : j + 1] for j in range(5)], axis=1).reshape(CH)
    bg_ref[...] = jnp.concatenate([totals[5 + j : 6 + j] for j in range(5)], axis=1).reshape(CH)

    def from_me(g, i):
        p1, p2, p3 = order[g]
        return (p1 == z) & (p2 == x) & (p3 == i) & (c == ylo)

    for g in range(3):
        for i in range(4):
            @pl.when(jnp.logical_not(from_me(g, i)))
            def _():
                rcopy(y2s.at[g, 0], y2r.at[g, i], y2_ss.at[4 * g], y2_rs.at[4 * g + i], sib).wait_recv()

        total = slot_sum(y2r[g])
        for dc in range(3):
            wg_ref[3 * g + dc] = total[:, 80 * dc : 80 * (dc + 1)]

    sp_drain(*bst)
    rcopy(gb_most, gb_most, gb2_ss.at[0], gb2_rs.at[0], sib).wait_send()
    for g in range(3):
        for j in range(4):
            @pl.when(jnp.logical_not(sum3_mine(g, j)))
            def _():
                sum3(g, j).wait_send()


def finish(*refs):
    count = (len(refs) - 1) // 2
    sems = refs[-1]
    copies = [pltpu.make_async_copy(refs[i], refs[count + i], sems.at[i]) for i in range(count)]
    for copy in copies:
        copy.start()
    for copy in copies:
        copy.wait()


def body(inputs, norm_gain, norm_bias, conv_weight, upstream):
    dma = pltpu.SemaphoreType.DMA
    vm = pltpu.VMEM
    scratch = [
        vm((2, NIMG, COLS, CH), BF16),
        vm((2, NIMG, COLS, CH), BF16),
        vm((4 * PIX, 3 * CH), BF16),
        vm((4 * PIX, 3 * CH), BF16),
        vm((2, 320, OWN), BF16),
        vm((9, CH, CH), BF16),
        vm((9, 320, CH), BF16),
        vm((9, 320, CH), BF16),
        vm((9, 4, 80, CH), BF16),
        vm((9, 80, CH), F32),
        vm((4, 80, CH), F32),
        vm((3, 3, 3, 80, CH), BF16),
        vm((3, CH, 256), BF16),
        vm((3, 3, 160, 256), BF16),
        vm((CH, 256), F32),
        vm((3, 160, 256), F32),
        vm((3, 4, 40, 256), F32),
        vm((3, 4, 40, 256), F32),
        vm((OWN, CH), F32),
        vm((2, 16, CH), F32),
        vm((2, 16, CH), F32),
        vm((16, 128), F32),
        vm((16, 16, 128), F32),
        vm((32, 128), F32),
        vm((16, 32, 128), F32),
        vm((8, 16, 128), F32),
        dma((1,)), dma((1,)),
        dma((1,)), dma((1,)),
        dma((1,)), dma((1,)),
        dma((4,)), dma((4,)),
        dma((14,)), dma((14,)),
        dma((12,)), dma((12,)),
        dma((5,)), dma((5,)),
        dma((9,)), dma((9,)),
        dma((9,)), dma((9,)),
        dma((9,)), dma((9,)),
        dma((12,)), dma((12,)),
    ]
    spec = pl.BlockSpec(memory_space=pltpu.VMEM)
    results = pl.pallas_call(
        kernel,
        out_shape=(
            jax.ShapeDtypeStruct(inputs.shape, BF16),
            jax.ShapeDtypeStruct(inputs.shape, BF16),
            jax.ShapeDtypeStruct((9, 40, 80), F32),
            jax.ShapeDtypeStruct((CH,), F32),
            jax.ShapeDtypeStruct((CH,), F32),
        ),
        in_specs=[spec] * 5,
        out_specs=(spec,) * 5,
        scratch_shapes=scratch,
        compiler_params=pltpu.CompilerParams(
            collective_id=0, has_side_effects=True, vmem_limit_bytes=62 * 2**20
        ),
        name="resblock",
    )(inputs, norm_gain, norm_bias, conv_weight, upstream)
    anywhere = pl.BlockSpec(memory_space=pl.ANY)
    mixed, input_grad, wg, gain_grad, bias_grad = pl.pallas_call(
        finish,
        out_shape=tuple(jax.ShapeDtypeStruct(r.shape, r.dtype) for r in results),
        in_specs=[spec] * 5,
        out_specs=(anywhere,) * 5,
        scratch_shapes=[dma((5,))],
        name="finish",
    )(*results)
    return (mixed, input_grad, wg.transpose(0, 2, 1), gain_grad, bias_grad)


def solution(mesh):
    in_specs = (
        P("dp", "space", None, None),
        P(),
        P(),
        P(None, "dp", None),
        P("dp", "space", None, None),
    )
    out_specs = (
        P("dp", "space", None, None),
        P("dp", "space", None, None),
        P(None, "dp", "space"),
        P(),
        P(),
    )
    return jax.shard_map(body, mesh=mesh, in_specs=in_specs, out_specs=out_specs, check_vma=False)
```
